256 devices in a mesh: lat: 32 (over x, z), lead: 8 (over y, core).
Axes of the slice: x: 4, y: 4, z: 8, core: 2. Of those that a mesh axis runs over, the one named last changes fastest.
Arguments:
- latent: bfloat16 [32, 256, 64, 256], P('lat', None, 'lead'), may hold values from -6 to 6
- conv_weight: bfloat16 [3, 3, 256, 256], replicated, may hold values from -0.125 to 0.125
- conv_bias: float32 [256], replicated, may hold values from -4 to 4
- norm_gain: float32 [256], replicated, may hold values from 0.1 to 1.9
- w_query: bfloat16 [256, 256], replicated, may hold values from -12 to 12
- w_key: bfloat16 [256, 256], replicated, may hold values from -0.25 to 0.25
- w_value: bfloat16 [256, 256], replicated, may hold values from -0.375 to 0.375
- w_out: bfloat16 [256, 256], replicated, may hold values from -0.375 to 0.375
Outputs:
- section_out: bfloat16 [32, 256, 64, 256], P('lat', None, 'lead')
The draws below stay inside these ranges and needn't reach their ends.
All inputs are finite; a program needn't handle non-finite values.
Results may differ from the reference program's by a relative error of at most 0.014.
Values may be sent and summed in bfloat16 or wider, within the bound.
No kernel may reach another device: no remote copies, remote signals or barrier semaphores. Data moves between devices by JAX's collectives and lax.ppermute only.
A program may use at most 128 MiB of HBM per device.

```python
import math
import jax
import jax.numpy as jnp
from jax import lax

C = 256
HD = 32
W = 256
NLAT = 32
L = 64


def key_matrix(key):
    limit = math.sqrt(C) / 4.0
    base = jax.random.truncated_normal(jax.random.fold_in(key, 21), -limit, limit, (C, C), jnp.float32)
    return base / math.sqrt(C)


def draw_w_key(key, part):
    return key_matrix(key).astype(jnp.bfloat16)


def draw_w_query(key, part):
    limit = math.sqrt(C) / 4.0
    base = jax.random.truncated_normal(jax.random.fold_in(key, 11), -limit, limit, (C, C), jnp.float32)
    return (base / math.sqrt(C)).astype(jnp.bfloat16)


def draw_latent(key, part):
    shape = (NLAT, W, L, C)
    return jax.random.truncated_normal(jax.random.fold_in(key, 34), -6.0, 6.0, shape, jnp.float32).astype(jnp.bfloat16)


def noise(own_key, dims, scale, most, held_as=jnp.bfloat16):
    result = scale * jax.random.normal(own_key, dims, jnp.float32)
    return jnp.clip(result, min=-most, max=most).astype(held_as)


def setup_inputs(seed: int = 0) -> dict:
    splits = jax.random.split(jax.random.key(seed), 9)
    return {
        "latent": draw_latent(jax.random.fold_in(splits[8], 71), 0),
        "conv_weight": noise(splits[1], (3, 3, C, C), (9 * C) ** -0.5, 0.125),
        "conv_bias": noise(splits[2], (C,), 1.0, 4.0, jnp.float32),
        "norm_gain": jnp.clip(1.0 + 0.18 * jax.random.normal(splits[3], (C,), jnp.float32), 0.1, 1.9),
        "w_query": draw_w_query(jax.random.fold_in(splits[8], 71), 0),
        "w_key": draw_w_key(jax.random.fold_in(splits[8], 71), 0),
        "w_value": noise(splits[6], (C, C), C ** -0.5, 0.375),
        "w_out": noise(splits[7], (C, C), C ** -0.5, 0.375),
    }


def section(rows, conv_weight, conv_bias, norm_gain, w_query, w_key, w_value, w_out):
    width = rows.shape[1] - 2
    leads = rows.shape[2]
    chans = rows.shape[3]
    acc = jnp.zeros((width * leads, chans), jnp.float32)
    for a in range(3):
        for b in range(3):
            piece = rows[a, b:b + width].reshape(-1, chans)
            acc = acc + jnp.dot(piece, conv_weight[a, b], preferred_element_type=jnp.float32)
    hidden = jax.nn.gelu(acc + conv_bias, approximate=True).astype(jnp.bfloat16)
    hf = hidden.astype(jnp.float32)
    mean = lax.optimization_barrier(jnp.mean(hf, axis=-1, keepdims=True))
    var = lax.optimization_barrier(jnp.mean((hf - mean) ** 2, axis=-1, keepdims=True))
    normed = ((hf - mean) * lax.rsqrt(var + 1e-05) * norm_gain).astype(jnp.bfloat16)
    query = jnp.dot(normed, w_query, preferred_element_type=jnp.float32).astype(jnp.bfloat16)
    keys = jnp.dot(normed, w_key, preferred_element_type=jnp.float32).astype(jnp.bfloat16)
    values = jnp.dot(normed, w_value, preferred_element_type=jnp.float32).astype(jnp.bfloat16)
    heads = chans // HD
    query = query.reshape(width, leads, heads, HD).astype(jnp.float32)
    keys = keys.reshape(width, leads, heads, HD).astype(jnp.float32)
    values = values.reshape(width, leads, heads, HD).astype(jnp.float32)
    scores = jnp.einsum('pqhd,pkhd->phqk', query, keys) / math.sqrt(HD)
    top = lax.optimization_barrier(jnp.max(scores, axis=-1, keepdims=True))
    expo = jnp.exp(scores - top)
    weights = (expo / lax.optimization_barrier(jnp.sum(expo, axis=-1, keepdims=True))).astype(jnp.bfloat16)
    attended = jnp.einsum('phqk,pkhd->pqhd', weights.astype(jnp.float32), values).astype(jnp.bfloat16)
    mixed = hidden.astype(jnp.float32) + jnp.dot(attended.reshape(-1, chans), w_out, preferred_element_type=jnp.float32)
    return mixed.astype(jnp.bfloat16).reshape(width, leads, chans)

def reference(latent, conv_weight, conv_bias, norm_gain, w_query, w_key, w_value, w_out):
    padded = jnp.pad(latent, ((1, 1), (1, 1), (0, 0), (0, 0)))

    def one_row(index):
        rows = lax.dynamic_slice_in_dim(padded, index, 3, 0)
        return section(rows, conv_weight, conv_bias, norm_gain, w_query, w_key, w_value, w_out)
    return lax.map(one_row, jnp.arange(latent.shape[0], dtype=jnp.int32))
```

```python
import functools
import math

import jax
import jax.numpy as jnp
from jax import lax
from jax.experimental import pallas as pl
from jax.experimental.pallas import tpu as pltpu
from jax.sharding import PartitionSpec as P

HD = 32
NT = (((1,), (1,)), ((), ()))
F32 = jnp.float32
BF16 = jnp.bfloat16
Q_SCALE = math.log2(math.e) / math.sqrt(HD)
VMEM = pl.BlockSpec(memory_space=pltpu.VMEM)


def params(mib):
    return pltpu.CompilerParams(vmem_limit_bytes=mib << 20)


def cost(flops, nbytes, transcendentals=0):
    return pl.CostEstimate(
        flops=int(flops), bytes_accessed=int(nbytes), transcendentals=int(transcendentals)
    )


def gelu(x):
    return 0.5 * x * (1.0 + jnp.tanh(math.sqrt(2 / math.pi) * (x + 0.044715 * (x * x * x))))


def layer_norm(hidden, gain):
    hidden = hidden.astype(F32)
    centred = hidden - jnp.mean(hidden, axis=-1, keepdims=True)
    var = jnp.mean(centred * centred, axis=-1, keepdims=True)
    return (centred * lax.rsqrt(var + 1e-05) * gain).astype(BF16)


def taps(ref, start, count):
    size, leads, chans = ref.shape
    zero = jnp.zeros((1, leads, chans), ref.dtype)
    out = []
    for first in (start - 1, start, start + 1):
        low, high = max(first, 0), min(first + count, size)
        piece = ref[low:high]
        if low > first:
            piece = jnp.concatenate([zero, piece], axis=0)
        if high < first + count:
            piece = jnp.concatenate([piece, zero], axis=0)
        out.append(piece.reshape(count * leads, chans))
    return out


def conv_kernel(tile, offset, shift, up, mid, down, weight, bias, gain, hidden_out, normed_out):
    width, leads, chans = hidden_out.shape
    rows = (up, mid.at[pl.ds(shift, up.shape[0])], down)

    def conv(i):
        pieces = [piece for row in rows for piece in taps(row, i * tile + offset, tile)]
        return jnp.dot(jnp.concatenate(pieces, axis=1), weight[...], preferred_element_type=F32)

    def finish(i, acc):
        here = slice(i * tile, (i + 1) * tile)
        hidden = gelu(acc + bias[...]).astype(BF16)
        hidden_out[here] = hidden.reshape(tile, leads, chans)
        normed_out[here] = layer_norm(hidden, gain[...]).reshape(tile, leads, chans)

    acc = conv(0)
    for i in range(width // tile):
        later = conv(i + 1) if (i + 1) * tile < width else None
        finish(i, acc)
        acc = later


def conv_norm(up, mid, down, weight, bias, gain, start, width):
    _, leads, chans = mid.shape
    low = max(start - 1, 0)
    tile = math.gcd(width, 32)
    shape = jax.ShapeDtypeStruct((width, leads, chans), BF16)
    size = width * leads * chans
    return pl.pallas_call(
        functools.partial(conv_kernel, tile, start - low, low),
        out_shape=[shape, shape],
        in_specs=[VMEM] * 6,
        out_specs=[VMEM] * 2,
        compiler_params=params(40),
        cost_estimate=cost(size * 18 * chans, size * 10 + 18 * chans * chans, size),
    )(up, mid, down, weight, bias, gain)


def attend_kernel(block, x_ref, w_ref, ones_ref, out_ref):
    parts, pixels, leads, chans = x_ref.shape
    times, heads = parts * leads, chans // HD
    lane = lax.broadcasted_iota(jnp.int32, (times, chans), 1)
    masks = [(lane >= h * HD) & (lane < (h + 1) * HD) for h in range(heads)]
    low_half = lax.broadcasted_iota(jnp.int32, (times, 2 * times), 1) < times

    def by_head(x):
        return jnp.concatenate([jnp.where(m, x, jnp.zeros_like(x)) for m in masks], axis=0)

    def soft(scores):
        out = []
        for i in range(heads // 2):
            pair = scores[:, 2 * times * i : 2 * times * (i + 1)]
            top0 = jnp.max(jnp.where(low_half, pair, -jnp.inf), axis=1, keepdims=True)
            top1 = jnp.max(jnp.where(low_half, -jnp.inf, pair), axis=1, keepdims=True)
            out.append(jnp.exp2(pair - jnp.where(low_half, top0, top1)).astype(BF16))
        return jnp.concatenate(out, axis=1)

    def body(i, carry):
        first = i * block
        x = x_ref[:, pl.ds(first, block)].reshape(parts * block * leads, chans)
        qkv = jnp.dot(x, w_ref[...], preferred_element_type=F32)
        shape = (parts, block, leads, chans)
        query = (qkv[:, :chans] * Q_SCALE).astype(BF16).reshape(shape)
        keys = qkv[:, chans : 2 * chans].astype(BF16).reshape(shape)
        values = qkv[:, 2 * chans :].astype(BF16).reshape(shape)

        def pick(a, p):
            return a[:, p].reshape(times, chans)

        scores = [
            lax.dot_general(pick(query, p), by_head(pick(keys, p)), NT, preferred_element_type=F32)
            for p in range(block)
        ]
        expo = [soft(s) for s in scores]
        total = jnp.dot(jnp.concatenate(expo, axis=0), ones_ref[...], preferred_element_type=F32)
        mixed = [
            jnp.dot(expo[p], by_head(pick(values, p)), preferred_element_type=F32)
            for p in range(block)
        ]
        for p in range(block):
            attended = mixed[p] / total[p * times : (p + 1) * times]
            out_ref[:, first + p] = attended.astype(BF16).reshape(parts, leads, chans)
        return carry

    lax.fori_loop(0, pixels // block, body, 0)


def attend(x, w_qkv, ones):
    parts, pixels, leads, chans = x.shape
    size = x.size
    return pl.pallas_call(
        functools.partial(attend_kernel, math.gcd(pixels, 8)),
        out_shape=jax.ShapeDtypeStruct(x.shape, BF16),
        in_specs=[VMEM] * 3,
        out_specs=VMEM,
        compiler_params=params(32),
        cost_estimate=cost(size * chans * 20, size * 4 + 6 * chans * chans, size * 2),
    )(x, w_qkv, ones)


def exchange(x):
    return lax.all_to_all(x, "lead", split_axis=0, concat_axis=0, tiled=True)


def shards(latent, conv_weight, conv_bias, norm_gain, w_query, w_key, w_value, w_out):
    latent = latent[0]
    width, leads, chans = latent.shape
    lats, parts = lax.axis_size("lat"), lax.axis_size("lead")
    times = parts * leads
    w_conv = conv_weight.reshape(9 * chans, chans)
    w_qkv = jnp.concatenate([w_query, w_key, w_value], axis=1)
    ones = (jnp.arange(chans // HD * times)[:, None] // times == jnp.arange(chans)[None] // HD).astype(BF16)
    bias, gain = conv_bias.reshape(1, chans), norm_gain.reshape(1, chans)
    north = [(i, i + 1) for i in range(lats - 1)]
    south = [(i + 1, i) for i in range(lats - 1)]

    up = lax.ppermute(latent, "lat", north)
    down = lax.ppermute(latent, "lat", south)
    hidden, normed = conv_norm(up, latent, down, w_conv, bias, gain, 0, width)
    block = exchange(normed.reshape(parts, width // parts, leads, chans))
    attended = exchange(attend(block, w_qkv, ones)).reshape(-1, chans)
    mixed = hidden.reshape(-1, chans).astype(F32) + jnp.dot(attended, w_out, preferred_element_type=F32)
    return mixed.astype(BF16).reshape(1, width, leads, chans)


def solution(mesh):
    in_specs = (P("lat", None, "lead", None), P(), P(), P(), P(), P(), P(), P())
    out_specs = P("lat", None, "lead", None)
    return jax.shard_map(shards, mesh=mesh, in_specs=in_specs, out_specs=out_specs, check_vma=False)
```

```python
import functools
import math

import jax
import jax.numpy as jnp
from jax import lax
from jax.experimental import pallas as pl
from jax.experimental.pallas import tpu as pltpu
from jax.sharding import PartitionSpec as P

HD = 32
NT = (((1,), (1,)), ((), ()))
F32 = jnp.float32
BF16 = jnp.bfloat16
Q_SCALE = math.log2(math.e) / math.sqrt(HD)
VMEM = pl.BlockSpec(memory_space=pltpu.VMEM)
SMEM = pl.BlockSpec(memory_space=pltpu.SMEM)
ANY = pl.BlockSpec(memory_space=pl.ANY)
WIDTHS = (128, 128)


def in_vmem(*arrays):
    return [pltpu.with_memory_space_constraint(x, pltpu.VMEM) for x in arrays]


def params(mib):
    return pltpu.CompilerParams(vmem_limit_bytes=mib << 20)


def cost(flops, nbytes, transcendentals=0):
    return pl.CostEstimate(
        flops=int(flops), bytes_accessed=int(nbytes), transcendentals=int(transcendentals)
    )


def gelu(x):
    return 0.5 * x * (1.0 + jnp.tanh(math.sqrt(2 / math.pi) * (x + 0.044715 * (x * x * x))))


def layer_norm(hidden, gain):
    hidden = hidden.astype(F32)
    centred = hidden - jnp.mean(hidden, axis=-1, keepdims=True)
    var = jnp.mean(centred * centred, axis=-1, keepdims=True)
    return (centred * lax.rsqrt(var + 1e-05) * gain).astype(BF16)


def taps(ref, start, count):
    size, leads, chans = ref.shape
    zero = jnp.zeros((1, leads, chans), ref.dtype)
    out = []
    for first in (start - 1, start, start + 1):
        low, high = max(first, 0), min(first + count, size)
        piece = ref[low:high]
        if low > first:
            piece = jnp.concatenate([zero, piece], axis=0)
        if high < first + count:
            piece = jnp.concatenate([piece, zero], axis=0)
        out.append(piece.reshape(count * leads, chans))
    return jnp.concatenate(out, axis=1)


def row_weight(weight, row):
    return weight[3 * row : 3 * row + 3].reshape(3 * weight.shape[1], weight.shape[2])


def centre_kernel(tile, pieces, mid, weight, bias, out, *piece_refs):
    width, leads, chans = mid.shape
    for (low, high), piece in zip(pieces, piece_refs):
        piece[...] = mid[low:high]
    for i in range(width // tile):
        acc = jnp.dot(taps(mid, i * tile, tile), row_weight(weight, 1), preferred_element_type=F32)
        out[i * tile * leads : (i + 1) * tile * leads] = acc + bias[...]


def centre_conv(mid, weight, bias, pieces):
    width, leads, chans = mid.shape
    rows = width * leads
    return pl.pallas_call(
        functools.partial(centre_kernel, 32, pieces),
        out_shape=[pltpu.VMEM((rows, chans), F32)]
        + [pltpu.VMEM((high - low, leads, chans), BF16) for low, high in pieces],
        in_specs=[VMEM] * 3,
        out_specs=[VMEM] * (1 + len(pieces)),
        compiler_params=params(8),
        cost_estimate=cost(rows * chans * 6 * chans, rows * chans * 6),
    )(mid, weight, bias)


def place(lead, parts, k):
    chip, core = lax.div(lead, 2), lax.rem(lead, 2)
    return 2 * lax.rem(chip + k // 2, parts // 2) + (core if k % 2 == 0 else 1 - core)


def conv_kernel(tile, offset, start, lats, ids, up, down, acc_in, weight, gain, hidden_out, *refs):
    normed_out, (hidden, normed) = refs[:-2], refs[-2:]
    width, leads, chans = hidden.shape
    parts = 2 * len(normed_out)
    first, last = ids[0] == 0, ids[0] == lats - 1

    def conv(i):
        high, low = taps(up, i * tile + offset, tile), taps(down, i * tile + offset, tile)
        high = jnp.where(first, jnp.zeros_like(high), high)
        low = jnp.where(last, jnp.zeros_like(low), low)
        acc = jnp.dot(high, row_weight(weight, 0), preferred_element_type=F32)
        return acc + jnp.dot(low, row_weight(weight, 2), preferred_element_type=F32)

    def finish(i, acc):
        here = slice(i * tile, (i + 1) * tile)
        begin = (start + i * tile) * leads
        value = gelu(acc + acc_in[begin : begin + tile * leads]).astype(BF16)
        normed[here] = layer_norm(value, gain[...]).reshape(tile, leads, chans)
        hidden[here] = value.reshape(tile, leads, chans)

    acc = conv(0)
    for i in range(width // tile):
        later = conv(i + 1) if (i + 1) * tile < width else None
        finish(i, acc)
        acc = later
    count = width // parts
    for k in range(parts):
        there = pl.ds(place(ids[1], parts, k) * count, count)
        hidden_out[k] = hidden[there]
        normed_out[k // 2][k % 2] = normed[there]


def conv_norm(lats, parts, ids, up, down, acc, weight, gain, start, width):
    _, leads, chans = up.shape
    low = max(start - 1, 0)
    tile = math.gcd(width, 32)
    size = width * leads * chans
    part = (width // parts, leads, chans)
    out = pl.pallas_call(
        functools.partial(conv_kernel, tile, start - low, start, lats),
        out_shape=[pltpu.VMEM((parts, *part), BF16)]
        + [pltpu.VMEM((2, *part), BF16)] * (parts // 2),
        in_specs=[SMEM] + [VMEM] * 5,
        out_specs=[VMEM] * (1 + parts // 2),
        scratch_shapes=[pltpu.VMEM((width, leads, chans), BF16)] * 2,
        compiler_params=params(12),
        cost_estimate=cost(size * 12 * chans, size * 12, size),
    )(ids, *in_vmem(up, down, acc), weight, gain)
    return out[0], out[1:]


def attend_kernel(block, wq_ref, wk_ref, wv_ref, *refs):
    ones_ref, chips = refs[-1], len(refs) // 2 - 1
    near, far, outs = refs[:chips], refs[chips], refs[chips + 1 : -1]
    xs = [x for k in range(chips) for x in (near[k].at[0], far.at[k])]
    parts, (pixels, leads, chans) = len(xs), xs[0].shape
    times, heads = parts * leads, chans // HD
    lane = lax.broadcasted_iota(jnp.int32, (times, chans), 1)
    masks = [(lane >= h * HD) & (lane < (h + 1) * HD) for h in range(heads)]
    low_half = lax.broadcasted_iota(jnp.int32, (times, 2 * times), 1) < times
    for h in range(heads):
        ones_ref[h * times : (h + 1) * times] = masks[h].astype(F32).astype(BF16)

    def by_head(x):
        return jnp.concatenate([jnp.where(m, x, jnp.zeros_like(x)) for m in masks], axis=0)

    def soft(scores):
        out = []
        for i in range(heads // 2):
            pair = scores[:, 2 * times * i : 2 * times * (i + 1)]
            top0 = jnp.max(jnp.where(low_half, pair, -jnp.inf), axis=1, keepdims=True)
            top1 = jnp.max(jnp.where(low_half, -jnp.inf, pair), axis=1, keepdims=True)
            out.append(jnp.exp2(pair - jnp.where(low_half, top0, top1)).astype(BF16))
        return jnp.concatenate(out, axis=1)

    for i in range(pixels // block):
        first = i * block
        x = jnp.concatenate([x_ref[first : first + block] for x_ref in xs], axis=0)
        x = x.reshape(parts * block * leads, chans)

        def project(w_ref, scale=None):
            flat = jnp.dot(x, w_ref[...], preferred_element_type=F32)
            flat = (flat if scale is None else flat * scale).astype(BF16)
            rows = flat.reshape(parts, block, leads, chans)
            return [rows[:, p].reshape(times, chans) for p in range(block)]

        query, keys, values = project(wq_ref, Q_SCALE), project(wk_ref), project(wv_ref)
        scores = [
            lax.dot_general(q, by_head(k), NT, preferred_element_type=F32)
            for q, k in zip(query, keys)
        ]
        expo = [soft(s) for s in scores]
        total = jnp.dot(jnp.concatenate(expo, axis=0), ones_ref[...], preferred_element_type=F32)
        mixed = [jnp.dot(e, by_head(v), preferred_element_type=F32) for e, v in zip(expo, values)]
        for p in range(block):
            attended = mixed[p] / total[p * times : (p + 1) * times]
            attended = attended.astype(BF16).reshape(parts, leads, chans)
            for k in range(parts):
                outs[k // 2][k % 2, first + p] = attended[k]


def attend(near, far, w_query, w_key, w_value):
    chips, pixels, leads, chans = far.shape
    size, times = 2 * far.size, 2 * chips * leads
    return pl.pallas_call(
        functools.partial(attend_kernel, math.gcd(pixels, 8)),
        out_shape=[pltpu.VMEM(near[0].shape, BF16)] * chips,
        in_specs=[VMEM] * (4 + chips),
        out_specs=[VMEM] * chips,
        scratch_shapes=[pltpu.VMEM((chans // HD * times, chans), BF16)],
        compiler_params=params(16),
        cost_estimate=cost(size * chans * 20, size * 4 + 6 * chans * chans, size * 2),
    )(w_query, w_key, w_value, *in_vmem(*near, far))


def out_kernel(start, ids, hidden_ref, w_ref, *refs):
    out_hbm, held, sems = refs[-3:]
    parts, count, leads, chans = hidden_ref.shape
    near, far = refs[: parts // 2], refs[parts // 2]
    copies = []
    for k in range(parts):
        x = near[k // 2][0] if k % 2 == 0 else far[k // 2]
        acc = jnp.dot(x.reshape(count * leads, chans), w_ref[...], preferred_element_type=F32)
        acc = acc + hidden_ref[k].reshape(count * leads, chans).astype(F32)
        held[k] = acc.astype(BF16).reshape(count, leads, chans)
    for k in range(parts):
        there = pl.ds(start + place(ids[1], parts, k) * count, count)
        copies.append(pltpu.make_async_copy(held.at[k], out_hbm.at[there], sems.at[k]))
        copies[-1].start()
    for copy in copies:
        copy.wait()


def project_out(ids, near, far, hidden, w_out, whole, start, total):
    parts, _, leads, chans = hidden.shape
    args = [ids, *in_vmem(hidden), w_out, *in_vmem(*near, far)] + ([] if whole is None else [whole])
    return pl.pallas_call(
        functools.partial(out_kernel, start),
        out_shape=jax.ShapeDtypeStruct((total, leads, chans), BF16),
        in_specs=[SMEM] + [VMEM] * (3 + len(near)) + ([] if whole is None else [ANY]),
        out_specs=ANY,
        scratch_shapes=[pltpu.VMEM(hidden.shape, BF16), pltpu.SemaphoreType.DMA((parts,))],
        input_output_aliases={} if whole is None else {4 + len(near): 0},
        compiler_params=params(8),
        cost_estimate=cost(hidden.size * 2 * chans, hidden.size * 6),
    )(*args)


def gather_kernel(*refs):
    for k, ref in enumerate(refs[:-1]):
        refs[-1][k] = ref[1]


def ship(pieces, sign):
    chips = len(pieces)
    near = [pieces[0]] + [
        lax.ppermute(
            pieces[k], "lead", [(i, (i + 2 * sign * k) % (2 * chips)) for i in range(2 * chips)]
        )
        for k in range(1, chips)
    ]
    part = pieces[0].shape[1:]
    others = pl.pallas_call(
        gather_kernel,
        out_shape=pltpu.VMEM((chips, *part), BF16),
        in_specs=[VMEM] * chips,
        out_specs=VMEM,
        compiler_params=params(4),
        cost_estimate=cost(0, chips * pieces[0].size * 2),
    )(*in_vmem(*near))
    return near, lax.ppermute(others, "lead", [(i, i ^ 1) for i in range(2 * chips)])


def shards(latent, conv_weight, conv_bias, norm_gain, w_query, w_key, w_value, w_out):
    latent = latent[0]
    width, leads, chans = latent.shape
    lats, parts = lax.axis_size("lat"), lax.axis_size("lead")
    w_conv = conv_weight.reshape(9, chans, chans)
    bias, gain = conv_bias.reshape(1, chans), norm_gain.reshape(1, chans)
    north = [(i, (i + 1) % lats) for i in range(lats)]
    south = [(i, (i - 1) % lats) for i in range(lats)]
    ids = jnp.stack([lax.axis_index("lat"), lax.axis_index("lead")])

    starts = [sum(WIDTHS[:i]) for i in range(len(WIDTHS))]
    ranges = [(max(i - 1, 0), min(i + n + 1, width)) for i, n in zip(starts, WIDTHS)]
    acc, *pieces = centre_conv(latent, w_conv, bias, ranges[1:])
    sides = [
        (lax.ppermute(piece, "lat", north), lax.ppermute(piece, "lat", south))
        for piece in [latent[: ranges[0][1]], *pieces]
    ]
    hiddens, blocks = [], []
    for (up, down), start, count in zip(sides, starts, WIDTHS):
        hidden, normed = conv_norm(lats, parts, ids, up, down, acc, w_conv, gain, start, count)
        hiddens.append(hidden)
        blocks.append(ship(normed, 1))
    backs = [ship(attend(*block, w_query, w_key, w_value), -1) for block in blocks]
    out = None
    for back, hidden, start in zip(backs, hiddens, starts):
        out = project_out(ids, *back, hidden, w_out, out, start, width)
    return out[None]


def solution(mesh):
    in_specs = (P("lat", None, "lead", None), P(), P(), P(), P(), P(), P(), P())
    out_specs = P("lat", None, "lead", None)
    return jax.shard_map(shards, mesh=mesh, in_specs=in_specs, out_specs=out_specs, check_vma=False)
```

```python
import functools
import math

import jax
import jax.numpy as jnp
from jax import lax
from jax.experimental import pallas as pl
from jax.experimental.pallas import tpu as pltpu
from jax.sharding import PartitionSpec as P

HD = 32
NT = (((1,), (1,)), ((), ()))
F32 = jnp.float32
BF16 = jnp.bfloat16
Q_SCALE = math.log2(math.e) / math.sqrt(HD)
VMEM = pl.BlockSpec(memory_space=pltpu.VMEM)
SMEM = pl.BlockSpec(memory_space=pltpu.SMEM)
ANY = pl.BlockSpec(memory_space=pl.ANY)
WIDTHS = (128, 128)


def in_vmem(*arrays):
    return [pltpu.with_memory_space_constraint(x, pltpu.VMEM) for x in arrays]


def params(mib):
    return pltpu.CompilerParams(vmem_limit_bytes=mib << 20)


def cost(flops, nbytes, transcendentals=0):
    return pl.CostEstimate(
        flops=int(flops), bytes_accessed=int(nbytes), transcendentals=int(transcendentals)
    )


def gelu(x):
    return 0.5 * x * (1.0 + jnp.tanh(math.sqrt(2 / math.pi) * (x + 0.044715 * (x * x * x))))


def layer_norm(hidden, gain):
    hidden = hidden.astype(F32)
    centred = hidden - jnp.mean(hidden, axis=-1, keepdims=True)
    var = jnp.mean(centred * centred, axis=-1, keepdims=True)
    return (centred * lax.rsqrt(var + 1e-05) * gain).astype(BF16)


def taps(ref, start, count):
    size, leads, chans = ref.shape
    zero = jnp.zeros((1, leads, chans), ref.dtype)
    out = []
    for first in (start - 1, start, start + 1):
        low, high = max(first, 0), min(first + count, size)
        piece = ref[low:high]
        if low > first:
            piece = jnp.concatenate([zero, piece], axis=0)
        if high < first + count:
            piece = jnp.concatenate([piece, zero], axis=0)
        out.append(piece.reshape(count * leads, chans))
    return jnp.concatenate(out, axis=1)


def head_kernel(src, dst, sem):
    copy = pltpu.make_async_copy(src.at[pl.ds(0, dst.shape[0])], dst, sem)
    copy.start()
    copy.wait()


def head(x, count):
    return pl.pallas_call(
        head_kernel,
        out_shape=pltpu.VMEM((count, *x.shape[1:]), x.dtype),
        in_specs=[ANY],
        out_specs=VMEM,
        scratch_shapes=[pltpu.SemaphoreType.DMA],
        compiler_params=params(4),
        cost_estimate=cost(0, x.size * 2),
    )(pltpu.with_memory_space_constraint(x, pltpu.HBM))


def row_weight(weight, row):
    return weight[3 * row : 3 * row + 3].reshape(3 * weight.shape[1], weight.shape[2])


def centre_kernel(tile, pieces, mid, weight, bias, out, *piece_refs):
    width, leads, chans = mid.shape
    for (low, high), piece in zip(pieces, piece_refs):
        piece[...] = mid[low:high]
    for i in range(width // tile):
        acc = jnp.dot(taps(mid, i * tile, tile), row_weight(weight, 1), preferred_element_type=F32)
        out[i * tile * leads : (i + 1) * tile * leads] = acc + bias[...]


def centre_conv(mid, weight, bias, pieces):
    width, leads, chans = mid.shape
    rows = width * leads
    return pl.pallas_call(
        functools.partial(centre_kernel, 32, pieces),
        out_shape=[pltpu.VMEM((rows, chans), F32)]
        + [pltpu.VMEM((high - low, leads, chans), BF16) for low, high in pieces],
        in_specs=[VMEM] * 3,
        out_specs=[VMEM] * (1 + len(pieces)),
        compiler_params=params(8),
        cost_estimate=cost(rows * chans * 6 * chans, rows * chans * 6),
    )(mid, weight, bias)


def place(lead, parts, k):
    chip, core = lax.div(lead, 2), lax.rem(lead, 2)
    return 2 * lax.rem(chip + k // 2, parts // 2) + (core if k % 2 == 0 else 1 - core)


def conv_kernel(tile, offset, start, lats, ids, down, up, acc_in, weight, gain, hidden_out, *refs):
    normed_out, (hidden, normed) = refs[:-2], refs[-2:]
    width, leads, chans = hidden.shape
    parts = 2 * len(normed_out)
    first, last = ids[0] == 0, ids[0] == lats - 1

    def conv(i):
        high, low = taps(up, i * tile + offset, tile), taps(down, i * tile + offset, tile)
        high = jnp.where(first, jnp.zeros_like(high), high)
        low = jnp.where(last, jnp.zeros_like(low), low)
        acc = jnp.dot(high, row_weight(weight, 0), preferred_element_type=F32)
        return acc + jnp.dot(low, row_weight(weight, 2), preferred_element_type=F32)

    def finish(i, acc):
        here = slice(i * tile, (i + 1) * tile)
        begin = (start + i * tile) * leads
        value = gelu(acc + acc_in[begin : begin + tile * leads]).astype(BF16)
        normed[here] = layer_norm(value, gain[...]).reshape(tile, leads, chans)
        hidden[here] = value.reshape(tile, leads, chans)

    acc = conv(0)
    for i in range(width // tile):
        later = conv(i + 1) if (i + 1) * tile < width else None
        finish(i, acc)
        acc = later
    count = width // parts
    for k in range(parts):
        there = pl.ds(place(ids[1], parts, k) * count, count)
        hidden_out[k] = hidden[there]
        normed_out[k // 2][k % 2] = normed[there]


def conv_norm(lats, parts, ids, up, down, acc, weight, gain, start, width):
    _, leads, chans = up.shape
    low = max(start - 1, 0)
    tile = math.gcd(width, 32)
    size = width * leads * chans
    part = (width // parts, leads, chans)
    out = pl.pallas_call(
        functools.partial(conv_kernel, tile, start - low, start, lats),
        out_shape=[pltpu.VMEM((parts, *part), BF16)]
        + [pltpu.VMEM((2, *part), BF16)] * (parts // 2),
        in_specs=[SMEM] + [VMEM] * 5,
        out_specs=[VMEM] * (1 + parts // 2),
        scratch_shapes=[pltpu.VMEM((width, leads, chans), BF16)] * 2,
        compiler_params=params(12),
        cost_estimate=cost(size * 12 * chans, size * 12, size),
    )(ids, *in_vmem(down, up, acc), weight, gain)
    return out[0], out[1:]


def attend_kernel(block, chips, wq_ref, wk_ref, wv_ref, *refs):
    ones_ref, outs, far, near = refs[-1], refs[-1 - chips : -1], refs[chips], refs[:chips]
    earlier = refs[chips + 1 : -1 - chips]
    for ref, out in zip(earlier, outs):
        out[:, : ref.shape[1]] = ref[...]
    behind = earlier[0].shape[1] if earlier else 0
    xs = [x for k in range(chips) for x in (near[k].at[0], far.at[k])]
    parts, (pixels, leads, chans) = len(xs), xs[0].shape
    times, heads = parts * leads, chans // HD
    lane = lax.broadcasted_iota(jnp.int32, (times, chans), 1)
    masks = [(lane >= h * HD) & (lane < (h + 1) * HD) for h in range(heads)]
    low_half = lax.broadcasted_iota(jnp.int32, (times, 2 * times), 1) < times
    for h in range(heads):
        ones_ref[h * times : (h + 1) * times] = masks[h].astype(F32).astype(BF16)

    def by_head(x):
        return jnp.concatenate([jnp.where(m, x, jnp.zeros_like(x)) for m in masks], axis=0)

    def soft(scores):
        out = []
        for i in range(heads // 2):
            pair = scores[:, 2 * times * i : 2 * times * (i + 1)]
            top0 = jnp.max(jnp.where(low_half, pair, -jnp.inf), axis=1, keepdims=True)
            top1 = jnp.max(jnp.where(low_half, -jnp.inf, pair), axis=1, keepdims=True)
            out.append(jnp.exp2(pair - jnp.where(low_half, top0, top1)).astype(BF16))
        return jnp.concatenate(out, axis=1)

    for i in range(pixels // block):
        first = i * block
        x = jnp.concatenate([x_ref[first : first + block] for x_ref in xs], axis=0)
        x = x.reshape(parts * block * leads, chans)

        def project(w_ref, scale=None):
            flat = jnp.dot(x, w_ref[...], preferred_element_type=F32)
            flat = (flat if scale is None else flat * scale).astype(BF16)
            rows = flat.reshape(parts, block, leads, chans)
            return [rows[:, p].reshape(times, chans) for p in range(block)]

        query, keys, values = project(wq_ref, Q_SCALE), project(wk_ref), project(wv_ref)
        scores = [
            lax.dot_general(q, by_head(k), NT, preferred_element_type=F32)
            for q, k in zip(query, keys)
        ]
        expo = [soft(s) for s in scores]
        total = jnp.dot(jnp.concatenate(expo, axis=0), ones_ref[...], preferred_element_type=F32)
        mixed = [jnp.dot(e, by_head(v), preferred_element_type=F32) for e, v in zip(expo, values)]
        for p in range(block):
            attended = mixed[p] / total[p * times : (p + 1) * times]
            attended = attended.astype(BF16).reshape(parts, leads, chans)
            for k in range(parts):
                outs[k // 2][k % 2, behind + first + p] = attended[k]


def attend(near, far, earlier, w_query, w_key, w_value):
    chips, pixels, leads, chans = far.shape
    size, times = 2 * far.size, 2 * chips * leads
    behind = earlier[0].shape[1] if earlier else 0
    return pl.pallas_call(
        functools.partial(attend_kernel, math.gcd(pixels, 8), chips),
        out_shape=[pltpu.VMEM((2, behind + pixels, leads, chans), BF16)] * chips,
        in_specs=[VMEM] * (4 + chips + len(earlier)),
        out_specs=[VMEM] * chips,
        scratch_shapes=[pltpu.VMEM((chans // HD * times, chans), BF16)],
        compiler_params=params(16),
        cost_estimate=cost(size * chans * 20, size * 4 + 6 * chans * chans, size * 2),
    )(w_query, w_key, w_value, *in_vmem(*near, far, *earlier))


def out_kernel(starts, core, chips, ids, w_ref, *refs):
    hiddens, refs = refs[: len(starts)], refs[len(starts) :]
    out_hbm, held, sems = refs[-3:]
    _, count, leads, chans = held.shape
    for i in range(chips):
        x = refs[i][0] if core == 0 else refs[0][i]
        hidden = jnp.concatenate([ref[2 * i + core] for ref in hiddens], axis=0)
        acc = jnp.dot(x.reshape(count * leads, chans), w_ref[...], preferred_element_type=F32)
        acc = acc + hidden.reshape(count * leads, chans).astype(F32)
        held[i] = acc.astype(BF16).reshape(count, leads, chans)
    copies = []
    for i in range(chips):
        low = 0
        for k, (start, ref) in enumerate(zip(starts, hiddens)):
            width = ref.shape[1]
            there = pl.ds(start + place(ids[1], 2 * chips, 2 * i + core) * width, width)
            copies.append(
                pltpu.make_async_copy(
                    held.at[i, pl.ds(low, width)], out_hbm.at[there], sems.at[k, i]
                )
            )
            copies[-1].start()
            low += width
    for copy in copies:
        copy.wait()


def project_out(core, ids, attended, hiddens, w_out, whole, starts, total):
    parts, _, leads, chans = hiddens[0].shape
    count = sum(hidden.shape[1] for hidden in hiddens)
    chips = parts // 2
    args = [ids, w_out, *in_vmem(*hiddens, *attended)] + ([] if whole is None else [whole])
    return pl.pallas_call(
        functools.partial(out_kernel, starts, core, chips),
        out_shape=jax.ShapeDtypeStruct((total, leads, chans), BF16),
        in_specs=[SMEM]
        + [VMEM] * (1 + len(hiddens) + len(attended))
        + ([] if whole is None else [ANY]),
        out_specs=ANY,
        scratch_shapes=[
            pltpu.VMEM((chips, count, leads, chans), BF16),
            pltpu.SemaphoreType.DMA((len(starts), chips)),
        ],
        input_output_aliases={} if whole is None else {len(args) - 1: 0},
        compiler_params=params(8),
        cost_estimate=cost(total * leads * chans * chans, total * leads * chans * 3),
    )(*args)


def gather_kernel(*refs):
    for k in range(refs[-1].shape[0]):
        refs[-1][k] = refs[k][1]


def send(pieces, sign):
    chips = len(pieces)
    return [pieces[0]] + [
        lax.ppermute(
            pieces[k], "lead", [(i, (i + 2 * sign * k) % (2 * chips)) for i in range(2 * chips)]
        )
        for k in range(1, chips)
    ]


def swap(near, *before):
    chips, part = len(near), near[0].shape[1:]
    others = pl.pallas_call(
        gather_kernel,
        out_shape=pltpu.VMEM((chips, *part), BF16),
        in_specs=[VMEM] * chips + [ANY] * len(before),
        out_specs=VMEM,
        compiler_params=params(4),
        cost_estimate=cost(0, chips * near[0].size * 2),
    )(*in_vmem(*near), *before)
    return lax.ppermute(others, "lead", [(i, i ^ 1) for i in range(2 * chips)])


def shards(latent, conv_weight, conv_bias, norm_gain, w_query, w_key, w_value, w_out):
    latent = latent[0]
    width, leads, chans = latent.shape
    lats, parts = lax.axis_size("lat"), lax.axis_size("lead")
    w_conv = conv_weight.reshape(9, chans, chans)
    bias, gain = conv_bias.reshape(1, chans), norm_gain.reshape(1, chans)
    north = [(i, (i + 1) % lats) for i in range(lats)]
    south = [(i, (i - 1) % lats) for i in range(lats)]
    ids = jnp.stack([lax.axis_index("lat"), lax.axis_index("lead")])

    starts = [sum(WIDTHS[:i]) for i in range(len(WIDTHS))]
    ranges = [(max(i - 1, 0), min(i + n + 1, width)) for i, n in zip(starts, WIDTHS)]
    acc, *pieces = centre_conv(latent, w_conv, bias, ranges[1:])
    sides = [
        (lax.ppermute(piece, "lat", north), lax.ppermute(piece, "lat", south))
        for piece in [head(latent, ranges[0][1]), *pieces]
    ]
    hiddens, arrived = [], []
    for (up, down), start, count in zip(sides, starts, WIDTHS):
        hidden, normed = conv_norm(lats, parts, ids, up, down, acc, w_conv, gain, start, count)
        hiddens.append(hidden)
        arrived.append(send(normed, 1))
    mixed, before = [], hiddens[-1]
    for near in arrived:
        far = swap(near, before)
        mixed = attend(near, far, mixed, w_query, w_key, w_value)
        before = mixed[0]
    near = send(mixed, -1)
    far = swap(near)
    out = project_out(0, ids, near, hiddens, w_out, None, starts, width)
    out = project_out(1, ids, [far], hiddens, w_out, out, starts, width)
    return out[None]


def solution(mesh):
    in_specs = (P("lat", None, "lead", None), P(), P(), P(), P(), P(), P(), P())
    out_specs = P("lat", None, "lead", None)
    return jax.shard_map(shards, mesh=mesh, in_specs=in_specs, out_specs=out_specs, check_vma=False)
```

```python
import functools
import math

import jax
import jax.numpy as jnp
from jax import lax
from jax.experimental import pallas as pl
from jax.experimental.pallas import tpu as pltpu
from jax.sharding import PartitionSpec as P

HD = 32
NT = (((1,), (1,)), ((), ()))
F32 = jnp.float32
BF16 = jnp.bfloat16
Q_SCALE = math.log2(math.e) / math.sqrt(HD)
VMEM = pl.BlockSpec(memory_space=pltpu.VMEM)
SMEM = pl.BlockSpec(memory_space=pltpu.SMEM)
ANY = pl.BlockSpec(memory_space=pl.ANY)
WIDTHS = (128, 128)


def in_vmem(*arrays):
    return [pltpu.with_memory_space_constraint(x, pltpu.VMEM) for x in arrays]


def params(mib):
    return pltpu.CompilerParams(vmem_limit_bytes=mib << 20)


def cost(flops, nbytes, transcendentals=0):
    return pl.CostEstimate(
        flops=int(flops), bytes_accessed=int(nbytes), transcendentals=int(transcendentals)
    )


def gelu(x):
    return 0.5 * x * (1.0 + jnp.tanh(math.sqrt(2 / math.pi) * (x + 0.044715 * (x * x * x))))


def layer_norm(hidden, gain):
    hidden = hidden.astype(F32)
    centred = hidden - jnp.mean(hidden, axis=-1, keepdims=True)
    var = jnp.mean(centred * centred, axis=-1, keepdims=True)
    return (centred * lax.rsqrt(var + 1e-05) * gain).astype(BF16)


def taps(ref, start, count):
    size, leads, chans = ref.shape
    zero = jnp.zeros((1, leads, chans), ref.dtype)
    out = []
    for first in (start - 1, start, start + 1):
        low, high = max(first, 0), min(first + count, size)
        piece = ref[low:high]
        if low > first:
            piece = jnp.concatenate([zero, piece], axis=0)
        if high < first + count:
            piece = jnp.concatenate([piece, zero], axis=0)
        out.append(piece.reshape(count * leads, chans))
    return jnp.concatenate(out, axis=1)


def head_kernel(src, dst, sems):
    count, ways = dst.shape[0], sems.shape[0]
    cuts = [count * i // ways for i in range(ways + 1)]
    copies = []
    for i, (low, high) in enumerate(zip(cuts, cuts[1:])):
        here = pl.ds(low, high - low)
        copies.append(pltpu.make_async_copy(src.at[here], dst.at[here], sems.at[i]))
        copies[-1].start()
    for copy in copies:
        copy.wait()


def head(x, count):
    return pl.pallas_call(
        head_kernel,
        out_shape=pltpu.VMEM((count, *x.shape[1:]), x.dtype),
        in_specs=[ANY],
        out_specs=VMEM,
        scratch_shapes=[pltpu.SemaphoreType.DMA((8,))],
        compiler_params=params(4),
        cost_estimate=cost(0, x.size * 2),
    )(pltpu.with_memory_space_constraint(x, pltpu.HBM))


def row_weight(weight, row):
    return weight[3 * row : 3 * row + 3].reshape(3 * weight.shape[1], weight.shape[2])


def centre_kernel(tile, pieces, mid, weight, bias, out, *piece_refs):
    width, leads, chans = mid.shape
    for (low, high), piece in zip(pieces, piece_refs):
        piece[...] = mid[low:high]
    for i in range(width // tile):
        acc = jnp.dot(taps(mid, i * tile, tile), row_weight(weight, 1), preferred_element_type=F32)
        out[i * tile * leads : (i + 1) * tile * leads] = acc + bias[...]


def centre_conv(mid, weight, bias, pieces):
    width, leads, chans = mid.shape
    rows = width * leads
    return pl.pallas_call(
        functools.partial(centre_kernel, 32, pieces),
        out_shape=[pltpu.VMEM((rows, chans), F32)]
        + [pltpu.VMEM((high - low, leads, chans), BF16) for low, high in pieces],
        in_specs=[VMEM] * 3,
        out_specs=[VMEM] * (1 + len(pieces)),
        compiler_params=params(8),
        cost_estimate=cost(rows * chans * 6 * chans, rows * chans * 6),
    )(mid, weight, bias)


def place(lead, parts, k):
    chip, core = lax.div(lead, 2), lax.rem(lead, 2)
    return 2 * lax.rem(chip + k // 2, parts // 2) + (core if k % 2 == 0 else 1 - core)


def conv_kernel(tile, offset, start, lats, ids, down, up, acc_in, weight, gain, hidden_out, *refs):
    normed_out, (hidden, normed) = refs[:-2], refs[-2:]
    width, leads, chans = hidden.shape
    parts = 2 * len(normed_out)
    first, last = ids[0] == 0, ids[0] == lats - 1

    def conv(i):
        high, low = taps(up, i * tile + offset, tile), taps(down, i * tile + offset, tile)
        high = jnp.where(first, jnp.zeros_like(high), high)
        low = jnp.where(last, jnp.zeros_like(low), low)
        acc = jnp.dot(high, row_weight(weight, 0), preferred_element_type=F32)
        return acc + jnp.dot(low, row_weight(weight, 2), preferred_element_type=F32)

    def finish(i, acc):
        here = slice(i * tile, (i + 1) * tile)
        begin = (start + i * tile) * leads
        value = gelu(acc + acc_in[begin : begin + tile * leads]).astype(BF16)
        normed[here] = layer_norm(value, gain[...]).reshape(tile, leads, chans)
        hidden[here] = value.reshape(tile, leads, chans)

    acc = conv(0)
    for i in range(width // tile):
        later = conv(i + 1) if (i + 1) * tile < width else None
        finish(i, acc)
        acc = later
    count = width // parts
    for k in range(parts):
        there = pl.ds(place(ids[1], parts, k) * count, count)
        hidden_out[k] = hidden[there]
        normed_out[k // 2][k % 2] = normed[there]


def conv_norm(lats, parts, ids, up, down, acc, weight, gain, start, width):
    _, leads, chans = up.shape
    low = max(start - 1, 0)
    tile = math.gcd(width, 32)
    size = width * leads * chans
    part = (width // parts, leads, chans)
    out = pl.pallas_call(
        functools.partial(conv_kernel, tile, start - low, start, lats),
        out_shape=[pltpu.VMEM((parts, *part), BF16)]
        + [pltpu.VMEM((2, *part), BF16)] * (parts // 2),
        in_specs=[SMEM] + [VMEM] * 5,
        out_specs=[VMEM] * (1 + parts // 2),
        scratch_shapes=[pltpu.VMEM((width, leads, chans), BF16)] * 2,
        compiler_params=params(12),
        cost_estimate=cost(size * 12 * chans, size * 12, size),
    )(ids, *in_vmem(down, up, acc), weight, gain)
    return out[0], out[1:]


def attend_kernel(block, chips, wq_ref, wk_ref, wv_ref, *refs):
    ones_ref, outs, far, near = refs[-1], refs[-1 - chips : -1], refs[chips], refs[:chips]
    xs = [x for k in range(chips) for x in (near[k].at[0], far.at[k])]
    parts, (pixels, leads, chans) = len(xs), xs[0].shape
    times, heads = parts * leads, chans // HD
    lane = lax.broadcasted_iota(jnp.int32, (times, chans), 1)
    masks = [(lane >= h * HD) & (lane < (h + 1) * HD) for h in range(heads)]
    low_half = lax.broadcasted_iota(jnp.int32, (times, 2 * times), 1) < times
    for h in range(heads):
        ones_ref[h * times : (h + 1) * times] = masks[h].astype(F32).astype(BF16)

    def by_head(x):
        return jnp.concatenate([jnp.where(m, x, jnp.zeros_like(x)) for m in masks], axis=0)

    def soft(scores):
        out = []
        for i in range(heads // 2):
            pair = scores[:, 2 * times * i : 2 * times * (i + 1)]
            top0 = jnp.max(jnp.where(low_half, pair, -jnp.inf), axis=1, keepdims=True)
            top1 = jnp.max(jnp.where(low_half, -jnp.inf, pair), axis=1, keepdims=True)
            out.append(jnp.exp2(pair - jnp.where(low_half, top0, top1)).astype(BF16))
        return jnp.concatenate(out, axis=1)

    for i in range(pixels // block):
        first = i * block
        x = jnp.concatenate([x_ref[first : first + block] for x_ref in xs], axis=0)
        x = x.reshape(parts * block * leads, chans)

        def project(w_ref, scale=None):
            flat = jnp.dot(x, w_ref[...], preferred_element_type=F32)
            flat = (flat if scale is None else flat * scale).astype(BF16)
            rows = flat.reshape(parts, block, leads, chans)
            return [rows[:, p].reshape(times, chans) for p in range(block)]

        query, keys, values = project(wq_ref, Q_SCALE), project(wk_ref), project(wv_ref)
        scores = [
            lax.dot_general(q, by_head(k), NT, preferred_element_type=F32)
            for q, k in zip(query, keys)
        ]
        expo = [soft(s) for s in scores]
        total = jnp.dot(jnp.concatenate(expo, axis=0), ones_ref[...], preferred_element_type=F32)
        mixed = [jnp.dot(e, by_head(v), preferred_element_type=F32) for e, v in zip(expo, values)]
        for p in range(block):
            attended = mixed[p] / total[p * times : (p + 1) * times]
            attended = attended.astype(BF16).reshape(parts, leads, chans)
            for k in range(parts):
                outs[k // 2][k % 2, first + p] = attended[k]


def attend(near, far, w_query, w_key, w_value):
    chips, pixels, leads, chans = far.shape
    size, times = 2 * far.size, 2 * chips * leads
    return pl.pallas_call(
        functools.partial(attend_kernel, math.gcd(pixels, 8), chips),
        out_shape=[pltpu.VMEM((2, pixels, leads, chans), BF16)] * chips,
        in_specs=[VMEM] * (4 + chips),
        out_specs=[VMEM] * chips,
        scratch_shapes=[pltpu.VMEM((chans // HD * times, chans), BF16)],
        compiler_params=params(16),
        cost_estimate=cost(size * chans * 20, size * 4 + 6 * chans * chans, size * 2),
    )(w_query, w_key, w_value, *in_vmem(*near, far))


def out_kernel(starts, core, chips, ids, w_ref, *refs):
    hiddens, refs = refs[: len(starts)], refs[len(starts) :]
    out_hbm, held, sems = refs[-3:]
    _, count, leads, chans = held.shape
    for i in range(chips):
        if core == 0:
            x = jnp.concatenate([refs[k * chips + i][0] for k in range(len(starts))], axis=0)
        else:
            x = refs[0][i]
        hidden = jnp.concatenate([ref[2 * i + core] for ref in hiddens], axis=0)
        acc = jnp.dot(x.reshape(count * leads, chans), w_ref[...], preferred_element_type=F32)
        acc = acc + hidden.reshape(count * leads, chans).astype(F32)
        held[i] = acc.astype(BF16).reshape(count, leads, chans)
    copies = []
    for i in range(chips):
        low = 0
        for k, (start, ref) in enumerate(zip(starts, hiddens)):
            width = ref.shape[1]
            there = pl.ds(start + place(ids[1], 2 * chips, 2 * i + core) * width, width)
            copies.append(
                pltpu.make_async_copy(
                    held.at[i, pl.ds(low, width)], out_hbm.at[there], sems.at[k, i]
                )
            )
            copies[-1].start()
            low += width
    for copy in copies:
        copy.wait()


def project_out(core, ids, attended, hiddens, w_out, whole, starts, total):
    parts, _, leads, chans = hiddens[0].shape
    count = sum(hidden.shape[1] for hidden in hiddens)
    chips = parts // 2
    args = [ids, w_out, *in_vmem(*hiddens, *attended)] + ([] if whole is None else [whole])
    return pl.pallas_call(
        functools.partial(out_kernel, starts, core, chips),
        out_shape=jax.ShapeDtypeStruct((total, leads, chans), BF16),
        in_specs=[SMEM]
        + [VMEM] * (1 + len(hiddens) + len(attended))
        + ([] if whole is None else [ANY]),
        out_specs=ANY,
        scratch_shapes=[
            pltpu.VMEM((chips, count, leads, chans), BF16),
            pltpu.SemaphoreType.DMA((len(starts), chips)),
        ],
        input_output_aliases={} if whole is None else {len(args) - 1: 0},
        compiler_params=params(8),
        cost_estimate=cost(total * leads * chans * chans, total * leads * chans * 3),
    )(*args)


def gather_kernel(chunks, chips, *refs):
    out, low = refs[-1], 0
    for near in [refs[i * chips : (i + 1) * chips] for i in range(chunks)]:
        width = near[0].shape[1]
        for k, ref in enumerate(near):
            out[k, low : low + width] = ref[1]
        low += width


def send(pieces, sign):
    chips = len(pieces)
    return [pieces[0]] + [
        lax.ppermute(
            pieces[k], "lead", [(i, (i + 2 * sign * k) % (2 * chips)) for i in range(2 * chips)]
        )
        for k in range(1, chips)
    ]


def swap(nears, *before):
    chips, leads, chans = len(nears[0]), *nears[0][0].shape[2:]
    count = sum(near[0].shape[1] for near in nears)
    flat = [x for near in nears for x in near]
    others = pl.pallas_call(
        functools.partial(gather_kernel, len(nears), chips),
        out_shape=pltpu.VMEM((chips, count, leads, chans), BF16),
        in_specs=[VMEM] * len(flat) + [ANY] * len(before),
        out_specs=VMEM,
        compiler_params=params(4),
        cost_estimate=cost(0, chips * count * leads * chans * 4),
    )(*in_vmem(*flat), *before)
    return lax.ppermute(others, "lead", [(i, i ^ 1) for i in range(2 * chips)])


def shards(latent, conv_weight, conv_bias, norm_gain, w_query, w_key, w_value, w_out):
    latent = latent[0]
    width, leads, chans = latent.shape
    lats, parts = lax.axis_size("lat"), lax.axis_size("lead")
    w_conv = conv_weight.reshape(9, chans, chans)
    bias, gain = conv_bias.reshape(1, chans), norm_gain.reshape(1, chans)
    north = [(i, (i + 1) % lats) for i in range(lats)]
    south = [(i, (i - 1) % lats) for i in range(lats)]
    ids = jnp.stack([lax.axis_index("lat"), lax.axis_index("lead")])

    starts = [sum(WIDTHS[:i]) for i in range(len(WIDTHS))]
    ranges = [(max(i - 1, 0), min(i + n + 1, width)) for i, n in zip(starts, WIDTHS)]
    acc, *pieces = centre_conv(latent, w_conv, bias, ranges[1:])
    sides = [
        (lax.ppermute(piece, "lat", north), lax.ppermute(piece, "lat", south))
        for piece in [head(latent, ranges[0][1]), *pieces]
    ]
    hiddens, arrived = [], []
    for (up, down), start, count in zip(sides, starts, WIDTHS):
        hidden, normed = conv_norm(lats, parts, ids, up, down, acc, w_conv, gain, start, count)
        hiddens.append(hidden)
        arrived.append(send(normed, 1))
    returned, before = [], hiddens[-1]
    for near in arrived:
        mixed = attend(near, swap([near], before), w_query, w_key, w_value)
        returned.append(send(mixed, -1))
        before = mixed[0]
    far = swap(returned)
    near = [x for pieces in returned for x in pieces]
    out = project_out(0, ids, near, hiddens, w_out, None, starts, width)
    out = project_out(1, ids, [far], hiddens, w_out, out, starts, width)
    return out[None]


def solution(mesh):
    in_specs = (P("lat", None, "lead", None), P(), P(), P(), P(), P(), P(), P())
    out_specs = P("lat", None, "lead", None)
    return jax.shard_map(shards, mesh=mesh, in_specs=in_specs, out_specs=out_specs, check_vma=False)
```

```python
import functools
import math

import jax
import jax.numpy as jnp
from jax import lax
from jax.experimental import pallas as pl
from jax.experimental.pallas import tpu as pltpu
from jax.sharding import PartitionSpec as P

HD = 32
NT = (((1,), (1,)), ((), ()))
F32 = jnp.float32
BF16 = jnp.bfloat16
Q_SCALE = math.log2(math.e) / math.sqrt(HD)
VMEM = pl.BlockSpec(memory_space=pltpu.VMEM)
SMEM = pl.BlockSpec(memory_space=pltpu.SMEM)
ANY = pl.BlockSpec(memory_space=pl.ANY)
WIDTHS = (128, 128)


def in_vmem(*arrays):
    return [pltpu.with_memory_space_constraint(x, pltpu.VMEM) for x in arrays]


def params(mib):
    return pltpu.CompilerParams(vmem_limit_bytes=mib << 20)


def cost(flops, nbytes, transcendentals=0):
    return pl.CostEstimate(
        flops=int(flops), bytes_accessed=int(nbytes), transcendentals=int(transcendentals)
    )


def gelu(x):
    return 0.5 * x * (1.0 + jnp.tanh(math.sqrt(2 / math.pi) * (x + 0.044715 * (x * x * x))))


def layer_norm(hidden, gain):
    hidden = hidden.astype(F32)
    centred = hidden - jnp.mean(hidden, axis=-1, keepdims=True)
    var = jnp.mean(centred * centred, axis=-1, keepdims=True)
    return (centred * lax.rsqrt(var + 1e-05) * gain).astype(BF16)


def taps(ref, start, count):
    size, leads, chans = ref.shape
    zero = jnp.zeros((1, leads, chans), ref.dtype)
    out = []
    for first in (start - 1, start, start + 1):
        low, high = max(first, 0), min(first + count, size)
        piece = ref[low:high]
        if low > first:
            piece = jnp.concatenate([zero, piece], axis=0)
        if high < first + count:
            piece = jnp.concatenate([piece, zero], axis=0)
        out.append(piece.reshape(count * leads, chans))
    return jnp.concatenate(out, axis=1)


def head_kernel(src, dst, sems):
    count, ways = dst.shape[0], sems.shape[0]
    cuts = [count * i // ways for i in range(ways + 1)]
    copies = []
    for i, (low, high) in enumerate(zip(cuts, cuts[1:])):
        here = pl.ds(low, high - low)
        copies.append(pltpu.make_async_copy(src.at[here], dst.at[here], sems.at[i]))
        copies[-1].start()
    for copy in copies:
        copy.wait()


def head(x, count):
    return pl.pallas_call(
        head_kernel,
        out_shape=pltpu.HBM((count, *x.shape[1:]), x.dtype),
        in_specs=[ANY],
        out_specs=ANY,
        scratch_shapes=[pltpu.SemaphoreType.DMA((8,))],
        compiler_params=params(4),
        cost_estimate=cost(0, x.size * 2),
    )(pltpu.with_memory_space_constraint(x, pltpu.HBM))


def row_weight(weight, row):
    return weight[3 * row : 3 * row + 3].reshape(3 * weight.shape[1], weight.shape[2])


def centre_kernel(tile, pieces, mid, weight, bias, out, *piece_refs):
    width, leads, chans = mid.shape
    for (low, high), piece in zip(pieces, piece_refs):
        piece[...] = mid[low:high]
    for i in range(width // tile):
        acc = jnp.dot(taps(mid, i * tile, tile), row_weight(weight, 1), preferred_element_type=F32)
        out[i * tile * leads : (i + 1) * tile * leads] = acc + bias[...]


def centre_conv(mid, weight, bias, pieces):
    width, leads, chans = mid.shape
    rows = width * leads
    return pl.pallas_call(
        functools.partial(centre_kernel, 32, pieces),
        out_shape=[pltpu.VMEM((rows, chans), F32)]
        + [pltpu.VMEM((high - low, leads, chans), BF16) for low, high in pieces],
        in_specs=[VMEM] * 3,
        out_specs=[VMEM] * (1 + len(pieces)),
        compiler_params=params(8),
        cost_estimate=cost(rows * chans * 6 * chans, rows * chans * 6),
    )(mid, weight, bias)


def place(lead, parts, k):
    chip = jnp.bitwise_and(lax.shift_right_logical(lead, 1) + k // 2, parts // 2 - 1)
    return 2 * chip + jnp.bitwise_xor(jnp.bitwise_and(lead, 1), k % 2)


def conv_kernel(tile, offset, start, lats, ids, down, up, acc_in, weight, gain, hidden_out, *refs):
    normed_out, (hidden, normed) = refs[:-2], refs[-2:]
    width, leads, chans = hidden.shape
    parts = 2 * len(normed_out)
    first, last = ids[0] == 0, ids[0] == lats - 1

    def conv(i):
        high, low = taps(up, i * tile + offset, tile), taps(down, i * tile + offset, tile)
        high = jnp.where(first, jnp.zeros_like(high), high)
        low = jnp.where(last, jnp.zeros_like(low), low)
        acc = jnp.dot(high, row_weight(weight, 0), preferred_element_type=F32)
        return acc + jnp.dot(low, row_weight(weight, 2), preferred_element_type=F32)

    def finish(i, acc):
        here = slice(i * tile, (i + 1) * tile)
        begin = (start + i * tile) * leads
        value = gelu(acc + acc_in[begin : begin + tile * leads]).astype(BF16)
        normed[here] = layer_norm(value, gain[...]).reshape(tile, leads, chans)
        hidden[here] = value.reshape(tile, leads, chans)

    acc = conv(0)
    for i in range(width // tile):
        later = conv(i + 1) if (i + 1) * tile < width else None
        finish(i, acc)
        acc = later
    count = width // parts
    for k in range(parts):
        there = pl.ds(place(ids[1], parts, k) * count, count)
        hidden_out[k] = hidden[there]
        normed_out[k // 2][k % 2] = normed[there]


def conv_norm(lats, parts, ids, up, down, acc, weight, gain, start, width):
    _, leads, chans = up.shape
    low = max(start - 1, 0)
    tile = math.gcd(width, 32)
    size = width * leads * chans
    part = (width // parts, leads, chans)
    out = pl.pallas_call(
        functools.partial(conv_kernel, tile, start - low, start, lats),
        out_shape=[pltpu.VMEM((parts, *part), BF16)]
        + [pltpu.VMEM((2, *part), BF16)] * (parts // 2),
        in_specs=[SMEM] + [VMEM] * 5,
        out_specs=[VMEM] * (1 + parts // 2),
        scratch_shapes=[pltpu.VMEM((width, leads, chans), BF16)] * 2,
        compiler_params=params(12),
        cost_estimate=cost(size * 12 * chans, size * 12, size),
    )(ids, *in_vmem(down, up, acc), weight, gain)
    return out[0], out[1:]


def attend_kernel(block, chips, wq_ref, wk_ref, wv_ref, *refs):
    ones_ref, outs, far, near = refs[-1], refs[-1 - chips : -1], refs[chips], refs[:chips]
    xs = [x for k in range(chips) for x in (near[k].at[0], far.at[k])]
    parts, (pixels, leads, chans) = len(xs), xs[0].shape
    times, heads = parts * leads, chans // HD
    lane = lax.broadcasted_iota(jnp.int32, (times, chans), 1)
    masks = [(lane >= h * HD) & (lane < (h + 1) * HD) for h in range(heads)]
    low_half = lax.broadcasted_iota(jnp.int32, (times, 2 * times), 1) < times
    for h in range(heads):
        ones_ref[h * times : (h + 1) * times] = masks[h].astype(F32).astype(BF16)

    def by_head(x):
        return jnp.concatenate([jnp.where(m, x, jnp.zeros_like(x)) for m in masks], axis=0)

    def soft(scores):
        out = []
        for i in range(heads // 2):
            pair = scores[:, 2 * times * i : 2 * times * (i + 1)]
            top0 = jnp.max(jnp.where(low_half, pair, -jnp.inf), axis=1, keepdims=True)
            top1 = jnp.max(jnp.where(low_half, -jnp.inf, pair), axis=1, keepdims=True)
            out.append(jnp.exp2(pair - jnp.where(low_half, top0, top1)).astype(BF16))
        return jnp.concatenate(out, axis=1)

    for i in range(pixels // block):
        first = i * block
        x = jnp.concatenate([x_ref[first : first + block] for x_ref in xs], axis=0)
        x = x.reshape(parts * block * leads, chans)

        def project(w_ref, scale=None):
            flat = jnp.dot(x, w_ref[...], preferred_element_type=F32)
            flat = (flat if scale is None else flat * scale).astype(BF16)
            rows = flat.reshape(parts, block, leads, chans)
            return [rows[:, p].reshape(times, chans) for p in range(block)]

        query, keys, values = project(wq_ref, Q_SCALE), project(wk_ref), project(wv_ref)
        scores = [
            lax.dot_general(q, by_head(k), NT, preferred_element_type=F32)
            for q, k in zip(query, keys)
        ]
        expo = [soft(s) for s in scores]
        total = jnp.dot(jnp.concatenate(expo, axis=0), ones_ref[...], preferred_element_type=F32)
        mixed = [jnp.dot(e, by_head(v), preferred_element_type=F32) for e, v in zip(expo, values)]
        for p in range(block):
            attended = mixed[p] / total[p * times : (p + 1) * times]
            attended = attended.astype(BF16).reshape(parts, leads, chans)
            for k in range(parts):
                outs[k // 2][k % 2, first + p] = attended[k]


def attend(near, far, w_query, w_key, w_value):
    chips, pixels, leads, chans = far.shape
    size, times = 2 * far.size, 2 * chips * leads
    return pl.pallas_call(
        functools.partial(attend_kernel, math.gcd(pixels, 16), chips),
        out_shape=[pltpu.VMEM((2, pixels, leads, chans), BF16)] * chips,
        in_specs=[VMEM] * (4 + chips),
        out_specs=[VMEM] * chips,
        scratch_shapes=[pltpu.VMEM((chans // HD * times, chans), BF16)],
        compiler_params=params(16),
        cost_estimate=cost(size * chans * 20, size * 4 + 6 * chans * chans, size * 2),
    )(w_query, w_key, w_value, *in_vmem(*near, far))


def out_kernel(starts, core, chips, ids, w_ref, *refs):
    hiddens, refs = refs[: len(starts)], refs[len(starts) :]
    out_hbm, held, sems = refs[-3:]
    _, count, leads, chans = held.shape
    for i in range(chips):
        if core == 0:
            x = jnp.concatenate([refs[k * chips + i][0] for k in range(len(starts))], axis=0)
        else:
            x = refs[0][i]
        hidden = jnp.concatenate([ref[2 * i + core] for ref in hiddens], axis=0)
        acc = jnp.dot(x.reshape(count * leads, chans), w_ref[...], preferred_element_type=F32)
        acc = acc + hidden.reshape(count * leads, chans).astype(F32)
        held[i] = acc.astype(BF16).reshape(count, leads, chans)
    copies = []
    for i in range(chips):
        low = 0
        for k, (start, ref) in enumerate(zip(starts, hiddens)):
            width = ref.shape[1]
            there = pl.ds(start + place(ids[1], 2 * chips, 2 * i + core) * width, width)
            copies.append(
                pltpu.make_async_copy(
                    held.at[i, pl.ds(low, width)], out_hbm.at[there], sems.at[k, i]
                )
            )
            copies[-1].start()
            low += width
    for copy in copies:
        copy.wait()


def project_out(core, ids, attended, hiddens, w_out, whole, starts, total):
    parts, _, leads, chans = hiddens[0].shape
    count = sum(hidden.shape[1] for hidden in hiddens)
    chips = parts // 2
    args = [ids, w_out, *in_vmem(*hiddens, *attended)] + ([] if whole is None else [whole])
    return pl.pallas_call(
        functools.partial(out_kernel, starts, core, chips),
        out_shape=jax.ShapeDtypeStruct((total, leads, chans), BF16),
        in_specs=[SMEM]
        + [VMEM] * (1 + len(hiddens) + len(attended))
        + ([] if whole is None else [ANY]),
        out_specs=ANY,
        scratch_shapes=[
            pltpu.VMEM((chips, count, leads, chans), BF16),
            pltpu.SemaphoreType.DMA((len(starts), chips)),
        ],
        input_output_aliases={} if whole is None else {len(args) - 1: 0},
        compiler_params=params(8),
        cost_estimate=cost(total * leads * chans * chans, total * leads * chans * 3),
    )(*args)


def gather_kernel(chunks, chips, *refs):
    out, low = refs[-1], 0
    for near in [refs[i * chips : (i + 1) * chips] for i in range(chunks)]:
        width = near[0].shape[1]
        for k, ref in enumerate(near):
            out[k, low : low + width] = ref[1]
        low += width


def send(pieces, sign):
    chips = len(pieces)
    return [pieces[0]] + [
        lax.ppermute(
            pieces[k], "lead", [(i, (i + 2 * sign * k) % (2 * chips)) for i in range(2 * chips)]
        )
        for k in range(1, chips)
    ]


def swap(nears, *before):
    chips, leads, chans = len(nears[0]), *nears[0][0].shape[2:]
    count = sum(near[0].shape[1] for near in nears)
    flat = [x for near in nears for x in near]
    others = pl.pallas_call(
        functools.partial(gather_kernel, len(nears), chips),
        out_shape=pltpu.VMEM((chips, count, leads, chans), BF16),
        in_specs=[VMEM] * len(flat) + [ANY] * len(before),
        out_specs=VMEM,
        compiler_params=params(4),
        cost_estimate=cost(0, chips * count * leads * chans * 4),
    )(*in_vmem(*flat), *before)
    return lax.ppermute(others, "lead", [(i, i ^ 1) for i in range(2 * chips)])


def shards(latent, conv_weight, conv_bias, norm_gain, w_query, w_key, w_value, w_out):
    latent = latent[0]
    width, leads, chans = latent.shape
    lats, parts = lax.axis_size("lat"), lax.axis_size("lead")
    w_conv = conv_weight.reshape(9, chans, chans)
    bias, gain = conv_bias.reshape(1, chans), norm_gain.reshape(1, chans)
    north = [(i, (i + 1) % lats) for i in range(lats)]
    south = [(i, (i - 1) % lats) for i in range(lats)]
    ids = jnp.stack([lax.axis_index("lat"), lax.axis_index("lead")])

    starts = [sum(WIDTHS[:i]) for i in range(len(WIDTHS))]
    ranges = [(max(i - 1, 0), min(i + n + 1, width)) for i, n in zip(starts, WIDTHS)]
    acc, *pieces = centre_conv(latent, w_conv, bias, ranges[1:])
    sides = [
        (lax.ppermute(piece, "lat", north), lax.ppermute(piece, "lat", south))
        for piece in [head(latent, ranges[0][1]), *pieces]
    ]
    hiddens, arrived = [], []
    for (up, down), start, count in zip(sides, starts, WIDTHS):
        hidden, normed = conv_norm(lats, parts, ids, up, down, acc, w_conv, gain, start, count)
        hiddens.append(hidden)
        arrived.append(send(normed, 1))
    returned, before = [], hiddens[-1]
    for near in arrived:
        mixed = attend(near, swap([near], before), w_query, w_key, w_value)
        returned.append(send(mixed, -1))
        before = mixed[0]
    far = swap(returned)
    near = [x for pieces in returned for x in pieces]
    out = project_out(0, ids, near, hiddens, w_out, None, starts, width)
    out = project_out(1, ids, [far], hiddens, w_out, out, starts, width)
    return out[None]


def solution(mesh):
    in_specs = (P("lat", None, "lead", None), P(), P(), P(), P(), P(), P(), P())
    out_specs = P("lat", None, "lead", None)
    return jax.shard_map(shards, mesh=mesh, in_specs=in_specs, out_specs=out_specs, check_vma=False)
```

```python
import functools
import math

import jax
import jax.numpy as jnp
from jax import lax
from jax.experimental import pallas as pl
from jax.experimental.pallas import tpu as pltpu
from jax.sharding import PartitionSpec as P

HD = 32
NT = (((1,), (1,)), ((), ()))
F32 = jnp.float32
BF16 = jnp.bfloat16
Q_SCALE = math.log2(math.e) / math.sqrt(HD)
VMEM = pl.BlockSpec(memory_space=pltpu.VMEM)
SMEM = pl.BlockSpec(memory_space=pltpu.SMEM)
ANY = pl.BlockSpec(memory_space=pl.ANY)
WIDTHS = (128, 128)


def in_vmem(*arrays):
    return [pltpu.with_memory_space_constraint(x, pltpu.VMEM) for x in arrays]


def params(mib):
    return pltpu.CompilerParams(vmem_limit_bytes=mib << 20)


def cost(flops, nbytes, transcendentals=0):
    return pl.CostEstimate(
        flops=int(flops), bytes_accessed=int(nbytes), transcendentals=int(transcendentals)
    )


def gelu(x):
    return 0.5 * x * (1.0 + jnp.tanh(math.sqrt(2 / math.pi) * (x + 0.044715 * (x * x * x))))


def layer_norm(hidden, gain):
    hidden = hidden.astype(F32)
    centred = hidden - jnp.mean(hidden, axis=-1, keepdims=True)
    var = jnp.mean(centred * centred, axis=-1, keepdims=True)
    return (centred * lax.rsqrt(var + 1e-05) * gain).astype(BF16)


def taps(ref, start, count):
    size, leads, chans = ref.shape
    zero = jnp.zeros((1, leads, chans), ref.dtype)
    out = []
    for first in (start - 1, start, start + 1):
        low, high = max(first, 0), min(first + count, size)
        piece = ref[low:high]
        if low > first:
            piece = jnp.concatenate([zero, piece], axis=0)
        if high < first + count:
            piece = jnp.concatenate([piece, zero], axis=0)
        out.append(piece.reshape(count * leads, chans))
    return jnp.concatenate(out, axis=1)


def head_kernel(src, dst, held, in_sems, out_sems):
    count, ways = dst.shape[0], in_sems.shape[0]
    cuts = [count * i // ways for i in range(ways + 1)]
    ins, outs = [], []
    for i, (low, high) in enumerate(zip(cuts, cuts[1:])):
        here = pl.ds(low, high - low)
        ins.append(pltpu.make_async_copy(src.at[here], held.at[here], in_sems.at[i]))
        outs.append(pltpu.make_async_copy(held.at[here], dst.at[here], out_sems.at[i]))
        ins[i].start()
    for i in range(ways):
        ins[i].wait()
        outs[i].start()
    for copy in outs:
        copy.wait()


def head(x, count):
    shape = (count, *x.shape[1:])
    return pl.pallas_call(
        head_kernel,
        out_shape=pltpu.HBM(shape, x.dtype),
        in_specs=[ANY],
        out_specs=ANY,
        scratch_shapes=[pltpu.VMEM(shape, x.dtype)] + [pltpu.SemaphoreType.DMA((4,))] * 2,
        compiler_params=params(4),
        cost_estimate=cost(0, x.size * 2),
    )(pltpu.with_memory_space_constraint(x, pltpu.HBM))


def row_weight(weight, row):
    return weight[3 * row : 3 * row + 3].reshape(3 * weight.shape[1], weight.shape[2])


def centre_kernel(tile, pieces, mid, weight, bias, out, *piece_refs):
    width, leads, chans = mid.shape
    for (low, high), piece in zip(pieces, piece_refs):
        piece[...] = mid[low:high]
    for i in range(width // tile):
        acc = jnp.dot(taps(mid, i * tile, tile), row_weight(weight, 1), preferred_element_type=F32)
        out[i * tile * leads : (i + 1) * tile * leads] = acc + bias[...]


def centre_conv(mid, weight, bias, pieces):
    width, leads, chans = mid.shape
    rows = width * leads
    return pl.pallas_call(
        functools.partial(centre_kernel, 32, pieces),
        out_shape=[pltpu.VMEM((rows, chans), F32)]
        + [pltpu.VMEM((high - low, leads, chans), BF16) for low, high in pieces],
        in_specs=[VMEM] * 3,
        out_specs=[VMEM] * (1 + len(pieces)),
        compiler_params=params(8),
        cost_estimate=cost(rows * chans * 6 * chans, rows * chans * 6),
    )(mid, weight, bias)


def place(lead, parts, k):
    chip = jnp.bitwise_and(lax.shift_right_logical(lead, 1) + k // 2, parts // 2 - 1)
    return 2 * chip + jnp.bitwise_xor(jnp.bitwise_and(lead, 1), k % 2)


def conv_kernel(tile, offset, start, lats, ids, down, up, acc_in, weight, gain, hidden_out, *refs):
    normed_out, (hidden, normed) = refs[:-2], refs[-2:]
    width, leads, chans = hidden.shape
    parts = 2 * len(normed_out)
    first, last = ids[0] == 0, ids[0] == lats - 1

    def conv(i):
        high, low = taps(up, i * tile + offset, tile), taps(down, i * tile + offset, tile)
        high = jnp.where(first, jnp.zeros_like(high), high)
        low = jnp.where(last, jnp.zeros_like(low), low)
        acc = jnp.dot(high, row_weight(weight, 0), preferred_element_type=F32)
        return acc + jnp.dot(low, row_weight(weight, 2), preferred_element_type=F32)

    def finish(i, acc):
        here = slice(i * tile, (i + 1) * tile)
        begin = (start + i * tile) * leads
        value = gelu(acc + acc_in[begin : begin + tile * leads]).astype(BF16)
        normed[here] = layer_norm(value, gain[...]).reshape(tile, leads, chans)
        hidden[here] = value.reshape(tile, leads, chans)

    acc = conv(0)
    for i in range(width // tile):
        later = conv(i + 1) if (i + 1) * tile < width else None
        finish(i, acc)
        acc = later
    count = width // parts
    for k in range(parts):
        there = pl.ds(place(ids[1], parts, k) * count, count)
        hidden_out[k] = hidden[there]
        normed_out[k // 2][k % 2] = normed[there]


def conv_norm(lats, parts, ids, up, down, acc, weight, gain, start, width):
    _, leads, chans = up.shape
    low = max(start - 1, 0)
    tile = math.gcd(width, 32)
    size = width * leads * chans
    part = (width // parts, leads, chans)
    out = pl.pallas_call(
        functools.partial(conv_kernel, tile, start - low, start, lats),
        out_shape=[pltpu.VMEM((parts, *part), BF16)]
        + [pltpu.VMEM((2, *part), BF16)] * (parts // 2),
        in_specs=[SMEM] + [VMEM] * 5,
        out_specs=[VMEM] * (1 + parts // 2),
        scratch_shapes=[pltpu.VMEM((width, leads, chans), BF16)] * 2,
        compiler_params=params(12),
        cost_estimate=cost(size * 12 * chans, size * 12, size),
    )(ids, *in_vmem(down, up, acc), weight, gain)
    return out[0], out[1:]


def attend_kernel(block, chips, wq_ref, wk_ref, wv_ref, *refs):
    ones_ref, outs, far, near = refs[-1], refs[-1 - chips : -1], refs[chips], refs[:chips]
    xs = [x for k in range(chips) for x in (near[k].at[0], far.at[k])]
    parts, (pixels, leads, chans) = len(xs), xs[0].shape
    times, heads = parts * leads, chans // HD
    lane = lax.broadcasted_iota(jnp.int32, (times, chans), 1)
    masks = [(lane >= h * HD) & (lane < (h + 1) * HD) for h in range(heads)]
    low_half = lax.broadcasted_iota(jnp.int32, (times, 2 * times), 1) < times
    for h in range(heads):
        ones_ref[h * times : (h + 1) * times] = masks[h].astype(F32).astype(BF16)

    def by_head(x):
        return jnp.concatenate([jnp.where(m, x, jnp.zeros_like(x)) for m in masks], axis=0)

    def soft(scores):
        out = []
        for i in range(heads // 2):
            pair = scores[:, 2 * times * i : 2 * times * (i + 1)]
            top0 = jnp.max(jnp.where(low_half, pair, -jnp.inf), axis=1, keepdims=True)
            top1 = jnp.max(jnp.where(low_half, -jnp.inf, pair), axis=1, keepdims=True)
            out.append(jnp.exp2(pair - jnp.where(low_half, top0, top1)).astype(BF16))
        return jnp.concatenate(out, axis=1)

    for i in range(pixels // block):
        first = i * block
        x = jnp.concatenate([x_ref[first : first + block] for x_ref in xs], axis=0)
        x = x.reshape(parts * block * leads, chans)

        def project(w_ref, scale=None):
            flat = jnp.dot(x, w_ref[...], preferred_element_type=F32)
            flat = (flat if scale is None else flat * scale).astype(BF16)
            rows = flat.reshape(parts, block, leads, chans)
            return [rows[:, p].reshape(times, chans) for p in range(block)]

        query, keys, values = project(wq_ref, Q_SCALE), project(wk_ref), project(wv_ref)
        scores = [
            lax.dot_general(q, by_head(k), NT, preferred_element_type=F32)
            for q, k in zip(query, keys)
        ]
        expo = [soft(s) for s in scores]
        total = jnp.dot(jnp.concatenate(expo, axis=0), ones_ref[...], preferred_element_type=F32)
        mixed = [jnp.dot(e, by_head(v), preferred_element_type=F32) for e, v in zip(expo, values)]
        for p in range(block):
            attended = mixed[p] / total[p * times : (p + 1) * times]
            attended = attended.astype(BF16).reshape(parts, leads, chans)
            for k in range(parts):
                outs[k // 2][k % 2, first + p] = attended[k]


def attend(near, far, w_query, w_key, w_value):
    chips, pixels, leads, chans = far.shape
    size, times = 2 * far.size, 2 * chips * leads
    return pl.pallas_call(
        functools.partial(attend_kernel, math.gcd(pixels, 16), chips),
        out_shape=[pltpu.VMEM((2, pixels, leads, chans), BF16)] * chips,
        in_specs=[VMEM] * (4 + chips),
        out_specs=[VMEM] * chips,
        scratch_shapes=[pltpu.VMEM((chans // HD * times, chans), BF16)],
        compiler_params=params(16),
        cost_estimate=cost(size * chans * 20, size * 4 + 6 * chans * chans, size * 2),
    )(w_query, w_key, w_value, *in_vmem(*near, far))


def out_kernel(starts, core, chips, ids, w_ref, *refs):
    hiddens, refs = refs[: len(starts)], refs[len(starts) :]
    out_hbm, held, sems = refs[-3:]
    _, count, leads, chans = held.shape
    copies = []
    for i in range(chips):
        if core == 0:
            x = jnp.concatenate([refs[k * chips + i][0] for k in range(len(starts))], axis=0)
        else:
            x = refs[0][i]
        hidden = jnp.concatenate([ref[2 * i + core] for ref in hiddens], axis=0)
        acc = jnp.dot(x.reshape(count * leads, chans), w_ref[...], preferred_element_type=F32)
        acc = acc + hidden.reshape(count * leads, chans).astype(F32)
        held[i] = acc.astype(BF16).reshape(count, leads, chans)
        low = 0
        for k, (start, ref) in enumerate(zip(starts, hiddens)):
            width = ref.shape[1]
            there = pl.ds(start + place(ids[1], 2 * chips, 2 * i + core) * width, width)
            copies.append(
                pltpu.make_async_copy(
                    held.at[i, pl.ds(low, width)], out_hbm.at[there], sems.at[k, i]
                )
            )
            copies[-1].start()
            low += width
    for copy in copies:
        copy.wait()


def project_out(core, ids, attended, hiddens, w_out, whole, starts, total):
    parts, _, leads, chans = hiddens[0].shape
    count = sum(hidden.shape[1] for hidden in hiddens)
    chips = parts // 2
    args = [ids, w_out, *in_vmem(*hiddens, *attended)] + ([] if whole is None else [whole])
    return pl.pallas_call(
        functools.partial(out_kernel, starts, core, chips),
        out_shape=jax.ShapeDtypeStruct((total, leads, chans), BF16),
        in_specs=[SMEM]
        + [VMEM] * (1 + len(hiddens) + len(attended))
        + ([] if whole is None else [ANY]),
        out_specs=ANY,
        scratch_shapes=[
            pltpu.VMEM((chips, count, leads, chans), BF16),
            pltpu.SemaphoreType.DMA((len(starts), chips)),
        ],
        input_output_aliases={} if whole is None else {len(args) - 1: 0},
        compiler_params=params(8),
        cost_estimate=cost(total * leads * chans * chans, total * leads * chans * 3),
    )(*args)


def gather_kernel(chunks, chips, *refs):
    out, low = refs[-1], 0
    for near in [refs[i * chips : (i + 1) * chips] for i in range(chunks)]:
        width = near[0].shape[1]
        for k, ref in enumerate(near):
            out[k, low : low + width] = ref[1]
        low += width


def send(pieces, sign):
    chips = len(pieces)
    return [pieces[0]] + [
        lax.ppermute(
            pieces[k], "lead", [(i, (i + 2 * sign * k) % (2 * chips)) for i in range(2 * chips)]
        )
        for k in range(1, chips)
    ]


def swap(nears, *before):
    chips, leads, chans = len(nears[0]), *nears[0][0].shape[2:]
    count = sum(near[0].shape[1] for near in nears)
    flat = [x for near in nears for x in near]
    others = pl.pallas_call(
        functools.partial(gather_kernel, len(nears), chips),
        out_shape=pltpu.VMEM((chips, count, leads, chans), BF16),
        in_specs=[VMEM] * len(flat) + [ANY] * len(before),
        out_specs=VMEM,
        compiler_params=params(4),
        cost_estimate=cost(0, chips * count * leads * chans * 4),
    )(*in_vmem(*flat), *before)
    return lax.ppermute(others, "lead", [(i, i ^ 1) for i in range(2 * chips)])


def shards(latent, conv_weight, conv_bias, norm_gain, w_query, w_key, w_value, w_out):
    latent = latent[0]
    width, leads, chans = latent.shape
    lats, parts = lax.axis_size("lat"), lax.axis_size("lead")
    w_conv = conv_weight.reshape(9, chans, chans)
    bias, gain = conv_bias.reshape(1, chans), norm_gain.reshape(1, chans)
    north = [(i, (i + 1) % lats) for i in range(lats)]
    south = [(i, (i - 1) % lats) for i in range(lats)]
    ids = jnp.stack([lax.axis_index("lat"), lax.axis_index("lead")])

    starts = [sum(WIDTHS[:i]) for i in range(len(WIDTHS))]
    ranges = [(max(i - 1, 0), min(i + n + 1, width)) for i, n in zip(starts, WIDTHS)]
    acc, *pieces = centre_conv(latent, w_conv, bias, ranges[1:])
    sides = [
        (lax.ppermute(piece, "lat", north), lax.ppermute(piece, "lat", south))
        for piece in [head(latent, ranges[0][1]), *pieces]
    ]
    hiddens, arrived = [], []
    for (up, down), start, count in zip(sides, starts, WIDTHS):
        hidden, normed = conv_norm(lats, parts, ids, up, down, acc, w_conv, gain, start, count)
        hiddens.append(hidden)
        arrived.append(send(normed, 1))
    returned, before = [], hiddens[-1]
    for near in arrived:
        mixed = attend(near, swap([near], before), w_query, w_key, w_value)
        returned.append(send(mixed, -1))
        before = mixed[0]
    far = swap(returned)
    near = [x for pieces in returned for x in pieces]
    out = project_out(0, ids, near, hiddens, w_out, None, starts, width)
    out = project_out(1, ids, [far], hiddens, w_out, out, starts, width)
    return out[None]


def solution(mesh):
    in_specs = (P("lat", None, "lead", None), P(), P(), P(), P(), P(), P(), P())
    out_specs = P("lat", None, "lead", None)
    return jax.shard_map(shards, mesh=mesh, in_specs=in_specs, out_specs=out_specs, check_vma=False)
```

```python
import functools
import math

import jax
import jax.numpy as jnp
from jax import lax
from jax.experimental import pallas as pl
from jax.experimental.pallas import tpu as pltpu
from jax.sharding import PartitionSpec as P

HD = 32
NT = (((1,), (1,)), ((), ()))
F32 = jnp.float32
BF16 = jnp.bfloat16
Q_SCALE = math.log2(math.e) / math.sqrt(HD)
VMEM = pl.BlockSpec(memory_space=pltpu.VMEM)
SMEM = pl.BlockSpec(memory_space=pltpu.SMEM)
ANY = pl.BlockSpec(memory_space=pl.ANY)
WIDTHS = (128, 128)


def in_vmem(*arrays):
    return [pltpu.with_memory_space_constraint(x, pltpu.VMEM) for x in arrays]


def params(mib):
    return pltpu.CompilerParams(vmem_limit_bytes=mib << 20)


def cost(flops, nbytes, transcendentals=0):
    return pl.CostEstimate(
        flops=int(flops), bytes_accessed=int(nbytes), transcendentals=int(transcendentals)
    )


def gelu(x):
    return 0.5 * x * (1.0 + jnp.tanh(math.sqrt(2 / math.pi) * (x + 0.044715 * (x * x * x))))


def layer_norm(hidden, gain):
    hidden = hidden.astype(F32)
    centred = hidden - jnp.mean(hidden, axis=-1, keepdims=True)
    var = jnp.mean(centred * centred, axis=-1, keepdims=True)
    return (centred * lax.rsqrt(var + 1e-05) * gain).astype(BF16)


def taps(ref, start, count):
    size, leads, chans = ref.shape
    zero = jnp.zeros((1, leads, chans), ref.dtype)
    out = []
    for first in (start - 1, start, start + 1):
        low, high = max(first, 0), min(first + count, size)
        piece = ref[low:high]
        if low > first:
            piece = jnp.concatenate([zero, piece], axis=0)
        if high < first + count:
            piece = jnp.concatenate([piece, zero], axis=0)
        out.append(piece.reshape(count * leads, chans))
    return jnp.concatenate(out, axis=1)


def head_kernel(src, dst, held, in_sems, out_sems):
    count, ways = dst.shape[0], in_sems.shape[0]
    cuts = [count * i // ways for i in range(ways + 1)]
    ins, outs = [], []
    for i, (low, high) in enumerate(zip(cuts, cuts[1:])):
        here = pl.ds(low, high - low)
        ins.append(pltpu.make_async_copy(src.at[here], held.at[here], in_sems.at[i]))
        outs.append(pltpu.make_async_copy(held.at[here], dst.at[here], out_sems.at[i]))
        ins[i].start()
    for i in range(ways):
        ins[i].wait()
        outs[i].start()
    for copy in outs:
        copy.wait()


def head(x, count):
    shape = (count, *x.shape[1:])
    return pl.pallas_call(
        head_kernel,
        out_shape=pltpu.HBM(shape, x.dtype),
        in_specs=[ANY],
        out_specs=ANY,
        scratch_shapes=[pltpu.VMEM(shape, x.dtype)] + [pltpu.SemaphoreType.DMA((4,))] * 2,
        compiler_params=params(4),
        cost_estimate=cost(0, x.size * 2),
    )(pltpu.with_memory_space_constraint(x, pltpu.HBM))


def row_weight(weight, row):
    return weight[3 * row : 3 * row + 3].reshape(3 * weight.shape[1], weight.shape[2])


def centre_kernel(tile, pieces, mid, weight, bias, out, *piece_refs):
    width, leads, chans = mid.shape
    for (low, high), piece in zip(pieces, piece_refs):
        piece[...] = mid[low:high]
    for i in range(width // tile):
        acc = jnp.dot(taps(mid, i * tile, tile), row_weight(weight, 1), preferred_element_type=F32)
        out[i * tile * leads : (i + 1) * tile * leads] = acc + bias[...]


def centre_conv(mid, weight, bias, pieces):
    width, leads, chans = mid.shape
    rows = width * leads
    return pl.pallas_call(
        functools.partial(centre_kernel, 32, pieces),
        out_shape=[pltpu.VMEM((rows, chans), F32)]
        + [pltpu.VMEM((high - low, leads, chans), BF16) for low, high in pieces],
        in_specs=[VMEM] * 3,
        out_specs=[VMEM] * (1 + len(pieces)),
        compiler_params=params(8),
        cost_estimate=cost(rows * chans * 6 * chans, rows * chans * 6),
    )(mid, weight, bias)


def place(lead, parts, k):
    chip = jnp.bitwise_and(lax.shift_right_logical(lead, 1) + k // 2, parts // 2 - 1)
    return 2 * chip + jnp.bitwise_xor(jnp.bitwise_and(lead, 1), k % 2)


def conv_kernel(tile, offset, start, lats, ids, down, up, acc_in, weight, gain, hidden_out, *refs):
    normed_out, (hidden, normed) = refs[:-2], refs[-2:]
    width, leads, chans = hidden.shape
    parts = 2 * len(normed_out)
    first, last = ids[0] == 0, ids[0] == lats - 1

    def conv(i):
        high, low = taps(up, i * tile + offset, tile), taps(down, i * tile + offset, tile)
        high = jnp.where(first, jnp.zeros_like(high), high)
        low = jnp.where(last, jnp.zeros_like(low), low)
        acc = jnp.dot(high, row_weight(weight, 0), preferred_element_type=F32)
        return acc + jnp.dot(low, row_weight(weight, 2), preferred_element_type=F32)

    def finish(i, acc):
        here = slice(i * tile, (i + 1) * tile)
        begin = (start + i * tile) * leads
        value = gelu(acc + acc_in[begin : begin + tile * leads]).astype(BF16)
        normed[here] = layer_norm(value, gain[...]).reshape(tile, leads, chans)
        hidden[here] = value.reshape(tile, leads, chans)

    acc = conv(0)
    for i in range(width // tile):
        later = conv(i + 1) if (i + 1) * tile < width else None
        finish(i, acc)
        acc = later
    count = width // parts
    for k in range(parts):
        there = pl.ds(place(ids[1], parts, k) * count, count)
        hidden_out[k] = hidden[there]
        normed_out[k // 2][k % 2] = normed[there]


def conv_norm(lats, parts, ids, up, down, acc, weight, gain, start, width):
    _, leads, chans = up.shape
    low = max(start - 1, 0)
    tile = math.gcd(width, 32)
    size = width * leads * chans
    part = (width // parts, leads, chans)
    out = pl.pallas_call(
        functools.partial(conv_kernel, tile, start - low, start, lats),
        out_shape=[pltpu.VMEM((parts, *part), BF16)]
        + [pltpu.VMEM((2, *part), BF16)] * (parts // 2),
        in_specs=[SMEM] + [VMEM] * 5,
        out_specs=[VMEM] * (1 + parts // 2),
        scratch_shapes=[pltpu.VMEM((width, leads, chans), BF16)] * 2,
        compiler_params=params(12),
        cost_estimate=cost(size * 12 * chans, size * 12, size),
    )(ids, *in_vmem(down, up, acc), weight, gain)
    return out[0], out[1:]


def attend_kernel(block, chips, wq_ref, wk_ref, wv_ref, *refs):
    ones_ref, outs, far, near = refs[-1], refs[-1 - chips : -1], refs[chips], refs[:chips]
    xs = [x for k in range(chips) for x in (near[k].at[0], far.at[k])]
    parts, (pixels, leads, chans) = len(xs), xs[0].shape
    times, heads = parts * leads, chans // HD
    lane = lax.broadcasted_iota(jnp.int32, (times, chans), 1)
    masks = [(lane >= h * HD) & (lane < (h + 1) * HD) for h in range(heads)]
    low_half = lax.broadcasted_iota(jnp.int32, (times, 2 * times), 1) < times
    for h in range(heads):
        ones_ref[h * times : (h + 1) * times] = masks[h].astype(F32).astype(BF16)

    def by_head(x):
        return jnp.concatenate([jnp.where(m, x, jnp.zeros_like(x)) for m in masks], axis=0)

    def soft(scores):
        out = []
        for i in range(heads // 2):
            pair = scores[:, 2 * times * i : 2 * times * (i + 1)]
            top0 = jnp.max(jnp.where(low_half, pair, -jnp.inf), axis=1, keepdims=True)
            top1 = jnp.max(jnp.where(low_half, -jnp.inf, pair), axis=1, keepdims=True)
            out.append(jnp.exp2(pair - jnp.where(low_half, top0, top1)).astype(BF16))
        return jnp.concatenate(out, axis=1)

    for i in range(pixels // block):
        first = i * block
        x = jnp.concatenate([x_ref[first : first + block] for x_ref in xs], axis=0)
        x = x.reshape(parts * block * leads, chans)

        def project(w_ref, scale=None):
            flat = jnp.dot(x, w_ref[...], preferred_element_type=F32)
            flat = (flat if scale is None else flat * scale).astype(BF16)
            rows = flat.reshape(parts, block, leads, chans)
            return [rows[:, p].reshape(times, chans) for p in range(block)]

        query, keys, values = project(wq_ref, Q_SCALE), project(wk_ref), project(wv_ref)
        scores = [
            lax.dot_general(q, by_head(k), NT, preferred_element_type=F32)
            for q, k in zip(query, keys)
        ]
        expo = [soft(s) for s in scores]
        total = jnp.dot(jnp.concatenate(expo, axis=0), ones_ref[...], preferred_element_type=F32)
        mixed = [jnp.dot(e, by_head(v), preferred_element_type=F32) for e, v in zip(expo, values)]
        for p in range(block):
            attended = mixed[p] / total[p * times : (p + 1) * times]
            attended = attended.astype(BF16).reshape(parts, leads, chans)
            for k in range(parts):
                outs[k // 2][k % 2, first + p] = attended[k]


def attend(near, far, w_query, w_key, w_value):
    chips, pixels, leads, chans = far.shape
    size, times = 2 * far.size, 2 * chips * leads
    return pl.pallas_call(
        functools.partial(attend_kernel, math.gcd(pixels, 16), chips),
        out_shape=[pltpu.VMEM((2, pixels, leads, chans), BF16)] * chips,
        in_specs=[VMEM] * (4 + chips),
        out_specs=[VMEM] * chips,
        scratch_shapes=[pltpu.VMEM((chans // HD * times, chans), BF16)],
        compiler_params=params(16),
        cost_estimate=cost(size * chans * 20, size * 4 + 6 * chans * chans, size * 2),
    )(w_query, w_key, w_value, *in_vmem(*near, far))


def out_kernel(starts, core, chips, ids, w_ref, *refs):
    hiddens, refs = refs[: len(starts)], refs[len(starts) :]
    out_hbm, held, sems = refs[-3:]
    _, count, leads, chans = held.shape
    copies = []
    for i in range(chips):
        if core == 0:
            x = jnp.concatenate([refs[k * chips + i][0] for k in range(len(starts))], axis=0)
        else:
            x = refs[0][i]
        hidden = jnp.concatenate([ref[2 * i + core] for ref in hiddens], axis=0)
        acc = jnp.dot(x.reshape(count * leads, chans), w_ref[...], preferred_element_type=F32)
        acc = acc + hidden.reshape(count * leads, chans).astype(F32)
        held[i] = acc.astype(BF16).reshape(count, leads, chans)
        low = 0
        for k, (start, ref) in enumerate(zip(starts, hiddens)):
            width = ref.shape[1]
            there = pl.ds(start + place(ids[1], 2 * chips, 2 * i + core) * width, width)
            copies.append(
                pltpu.make_async_copy(
                    held.at[i, pl.ds(low, width)], out_hbm.at[there], sems.at[k, i]
                )
            )
            copies[-1].start()
            low += width
    for copy in copies:
        copy.wait()


def project_out(core, ids, attended, hiddens, w_out, whole, starts, total):
    parts, _, leads, chans = hiddens[0].shape
    count = sum(hidden.shape[1] for hidden in hiddens)
    chips = parts // 2
    args = [ids, w_out, *in_vmem(*hiddens, *attended)] + ([] if whole is None else [whole])
    return pl.pallas_call(
        functools.partial(out_kernel, starts, core, chips),
        out_shape=jax.ShapeDtypeStruct((total, leads, chans), BF16),
        in_specs=[SMEM]
        + [VMEM] * (1 + len(hiddens) + len(attended))
        + ([] if whole is None else [ANY]),
        out_specs=ANY,
        scratch_shapes=[
            pltpu.VMEM((chips, count, leads, chans), BF16),
            pltpu.SemaphoreType.DMA((len(starts), chips)),
        ],
        input_output_aliases={} if whole is None else {len(args) - 1: 0},
        compiler_params=params(8),
        cost_estimate=cost(total * leads * chans * chans, total * leads * chans * 3),
    )(*args)


def farthest_first(chips):
    return [0] + sorted(range(1, chips), key=lambda k: abs(k - chips // 2))


def gather_kernel(chunks, chips, *refs):
    out, low = refs[-1], 0
    for near in [refs[i * chips : (i + 1) * chips] for i in range(chunks)]:
        width = near[0].shape[1]
        for k, ref in zip(farthest_first(chips), near):
            out[k, low : low + width] = ref[1]
        low += width


def send(pieces, sign):
    chips = len(pieces)
    return [pieces[0]] + [
        lax.ppermute(
            pieces[k], "lead", [(i, (i + 2 * sign * k) % (2 * chips)) for i in range(2 * chips)]
        )
        for k in range(1, chips)
    ]


def swap(nears, *before):
    chips, leads, chans = len(nears[0]), *nears[0][0].shape[2:]
    count = sum(near[0].shape[1] for near in nears)
    flat = [near[k] for near in nears for k in farthest_first(chips)]
    others = pl.pallas_call(
        functools.partial(gather_kernel, len(nears), chips),
        out_shape=pltpu.VMEM((chips, count, leads, chans), BF16),
        in_specs=[VMEM] * len(flat) + [ANY] * len(before),
        out_specs=VMEM,
        compiler_params=params(4),
        cost_estimate=cost(0, chips * count * leads * chans * 4),
    )(*in_vmem(*flat), *before)
    return lax.ppermute(others, "lead", [(i, i ^ 1) for i in range(2 * chips)])


def shards(latent, conv_weight, conv_bias, norm_gain, w_query, w_key, w_value, w_out):
    latent = latent[0]
    width, leads, chans = latent.shape
    lats, parts = lax.axis_size("lat"), lax.axis_size("lead")
    w_conv = conv_weight.reshape(9, chans, chans)
    bias, gain = conv_bias.reshape(1, chans), norm_gain.reshape(1, chans)
    north = [(i, (i + 1) % lats) for i in range(lats)]
    south = [(i, (i - 1) % lats) for i in range(lats)]
    ids = jnp.stack([lax.axis_index("lat"), lax.axis_index("lead")])

    starts = [sum(WIDTHS[:i]) for i in range(len(WIDTHS))]
    ranges = [(max(i - 1, 0), min(i + n + 1, width)) for i, n in zip(starts, WIDTHS)]
    acc, *pieces = centre_conv(latent, w_conv, bias, ranges[1:])
    sides = [
        (lax.ppermute(piece, "lat", north), lax.ppermute(piece, "lat", south))
        for piece in [head(latent, ranges[0][1]), *pieces]
    ]
    hiddens, arrived = [], []
    for (up, down), start, count in zip(sides, starts, WIDTHS):
        hidden, normed = conv_norm(lats, parts, ids, up, down, acc, w_conv, gain, start, count)
        hiddens.append(hidden)
        arrived.append(send(normed, 1))
    returned, before = [], hiddens[-1]
    for near in arrived:
        mixed = attend(near, swap([near], before), w_query, w_key, w_value)
        returned.append(send(mixed, -1))
        before = mixed[0]
    far = swap(returned)
    near = [x for pieces in returned for x in pieces]
    out = project_out(0, ids, near, hiddens, w_out, None, starts, width)
    out = project_out(1, ids, [far], hiddens, w_out, out, starts, width)
    return out[None]


def solution(mesh):
    in_specs = (P("lat", None, "lead", None), P(), P(), P(), P(), P(), P(), P())
    out_specs = P("lat", None, "lead", None)
    return jax.shard_map(shards, mesh=mesh, in_specs=in_specs, out_specs=out_specs, check_vma=False)
```
